32 devices in a mesh: grp: 4 (over z), row: 2 (over y), col: 4 (over x, core).
Axes of the slice: x: 2, y: 2, z: 4, core: 2. Of those that a mesh axis runs over, the one named last changes fastest.
Arguments:
- amplitudes: bfloat16 [1024, 16384], P(('grp', 'row'), 'col'), may hold values from -6 to 6
- ladder_ints: bfloat16 [16384, 16384], P('col', ('grp', 'row')), may hold values from -0.0625 to 0.0625
- tile_live: int32 [128, 128], P('col', ('grp', 'row')), may hold values 0 or 1
- cycle_direct: bfloat16 [4096, 4096], P('col', ('grp', 'row')), may hold values from -0.0625 to 0.0625
- cycle_exchange: bfloat16 [4096, 4096], P('col', ('grp', 'row')), may hold values from -0.0625 to 0.0625
- eps_occ: float32 [32], replicated, may hold values from -2 to -0.5
- eps_vir: float32 [128], replicated, may hold values from 0.5 to 3
Outputs:
- update: bfloat16 [1024, 16384], P('col', ('grp', 'row'))
The draws below stay inside these ranges and needn't reach their ends.
All inputs are finite; a program needn't handle non-finite values. No bound on the sum of `tile_live` on one device may be relied on, other than what follows from the above.
Results may differ from the reference program's by a relative error of at most 0.001.
Values may be sent and summed in bfloat16 or wider, within the bound.
A program may use at most 128 MiB of HBM per device.

```python
import jax
import jax.numpy as jnp

OCC = 32
VIR = 128
TILE = 128
OP = 1024
VP = 16384
PH = 4096


def place_ends(drawn, rng, smallest, high):
    shape = drawn.shape
    spot = [jax.random.randint(jax.random.fold_in(rng, axis), (), 0, shape[axis]) for axis in range(len(shape))]
    drawn = drawn.at[tuple(spot)].set(smallest)
    longest = shape.index(max(shape))
    spot[longest] = (spot[longest] + 1) % shape[longest]
    return drawn.at[tuple(spot)].set(high)


def block_levels(key, dims, pieces, low, high):
    def one(axis_at, blocks):
        heights = jax.random.uniform(jax.random.fold_in(jax.random.fold_in(key, 6), axis_at), (blocks,), jnp.float32, low / len(pieces), high / len(pieces))
        return jnp.repeat(jnp.exp(heights), dims[axis_at] // blocks).reshape((-1,) + (1,) * (len(dims) - axis_at - 1))

    factor_of = one(*pieces[0])
    for cut in pieces[1:]:
        factor_of = factor_of * one(*cut)
    return factor_of


def bell_draw(own_key, shape, width, bound, shards=(), held_as=jnp.bfloat16):
    drawn = width * jax.random.normal(own_key, shape, jnp.float32)
    if shards:
        drawn = drawn * block_levels(own_key, shape, shards, -0.22, 0.18)
    return jnp.clip(drawn, -bound, bound).astype(held_as)


def setup_inputs(seed: int = 0) -> dict:
    seeds = jax.random.split(jax.random.key(seed), 8)
    amplitudes = bell_draw(seeds[0], (OP, VP), 1.0, 6.0, ((0, 8), (1, 4)))
    ladder_ints = bell_draw(seeds[1], (VP, VP), (VP // 2) ** -0.5, 0.0625, ((0, 4), (1, 8)))
    tile_live = place_ends((jax.random.randint(seeds[2], (VP // TILE, VP // TILE), 0, 2) < 1).astype(jnp.int32), jax.random.fold_in(seeds[2], 1), 0, 1)
    cycle_direct = bell_draw(seeds[3], (PH, PH), (2 * PH) ** -0.5, 0.0625, ((0, 4), (1, 8)))
    cycle_exchange = bell_draw(seeds[4], (PH, PH), (2 * PH) ** -0.5, 0.0625, ((0, 4), (1, 8)))
    eps_occ = jnp.clip(jax.random.uniform(seeds[5], (OCC,), jnp.float32, -2.0, -0.5), -2.0, -0.5)
    eps_vir = jnp.clip(jax.random.uniform(seeds[6], (VIR,), jnp.float32, 0.5, 3.0), 0.5, 3.0)
    return {"amplitudes": amplitudes, "ladder_ints": ladder_ints, "tile_live": tile_live, "cycle_direct": cycle_direct, "cycle_exchange": cycle_exchange, "eps_occ": eps_occ, "eps_vir": eps_vir}


def reference(amplitudes, ladder_ints, tile_live, cycle_direct, cycle_exchange, eps_occ, eps_vir):
    expanded = jnp.repeat(jnp.repeat(tile_live, TILE, axis=0), TILE, axis=1).astype(jnp.bfloat16)
    masked = ladder_ints * expanded
    ladder = jnp.dot(amplitudes, masked, preferred_element_type=jnp.float32)
    amp_four = amplitudes.reshape(OCC, OCC, VIR, VIR)
    u_one = amp_four.transpose(0, 2, 1, 3).reshape(PH, PH)
    u_two = amp_four.transpose(0, 3, 1, 2).reshape(PH, PH)
    cycle = jnp.dot(cycle_direct, u_one, preferred_element_type=jnp.float32)
    cycle = cycle + jnp.dot(cycle_exchange, u_two, preferred_element_type=jnp.float32)
    cycle_pairs = cycle.reshape(OCC, VIR, OCC, VIR).transpose(0, 2, 1, 3).reshape(OP, VP)
    denom = (eps_vir[None, None, :, None] + eps_vir[None, None, None, :]
             - eps_occ[:, None, None, None] - eps_occ[None, :, None, None]).reshape(OP, VP)
    return ((ladder + cycle_pairs) / denom).astype(jnp.bfloat16)
```

```python
import functools

import jax
import jax.numpy as jnp
from jax import lax
from jax.experimental import pallas as pl
from jax.experimental.pallas import tpu as pltpu
from jax.sharding import PartitionSpec as P

LIMIT = 56 * 1024 * 1024
MESH = pl.DeviceIdType.MESH
CHUNK = 8


def fused_kernel(
    live_ref, occ_ref, vir_ref, row_ref, a_hbm, v_hbm, w_hbm, x_hbm, out_ref,
    vs, ab, a_own, w_own, w_split, w_mid, w_all, x_all, rhs_one, rhs_two, turn, part, cyc, exch, got_core, got_x, send_x, total,
    loc, loc_v, ss_up, ss_down, ss_row, rs_amp, ss_xg, rs_xg, ss_wg, rs_wg, ss_xc, rs_xc, ss_wc, rs_wc,
    ss_core, rs_core, ss_far, rs_far,
):
    f32, bf16 = jnp.float32, jnp.bfloat16
    depth, width = vs.shape
    zs, ys = lax.axis_size("grp"), lax.axis_size("row")
    cols = lax.axis_size("col")
    groups = zs * ys
    z, y, col = lax.axis_index("grp"), lax.axis_index("row"), lax.axis_index("col")
    grp = z * ys + y
    core, far = col % 2, col // 2
    vir = row_ref.shape[1]
    occ = occ_ref.shape[0]
    c_count = depth // vir
    a_count = width // vir
    chunks, all_rows = ab.shape[0], ab.shape[1]
    mine = all_rows // groups
    per_dev = mine // CHUNK
    i_count = occ // cols
    quarter = all_rows // cols
    edge = depth // live_ref.shape[0]

    def here(d_z=None, d_y=None, d_col=None):
        return (z if d_z is None else d_z, y if d_y is None else d_y, col if d_col is None else d_col)

    sibling = here(d_col=col + 1 - 2 * core)
    across = here(d_col=lax.rem(col + 2, cols))
    row_peer = here(d_y=1 - y)

    load_a = pltpu.make_async_copy(a_hbm, a_own, loc.at[0])
    load_a.start()
    load_w = pltpu.make_async_copy(w_hbm, w_own, loc.at[1])
    load_w.start()
    x_lanes = per_dev * vir
    own_x = pltpu.make_async_copy(
        x_hbm.at[:, pl.ds(pl.multiple_of(grp * a_count, a_count), a_count), :],
        x_all.at[col, :, :, pl.ds(pl.multiple_of(grp * x_lanes, x_lanes), x_lanes)],
        loc.at[2],
    )
    own_x.start()
    v_parts = loc_v.shape[0]
    v_rows = depth // v_parts

    def load_v(n):
        at = pl.ds(pl.multiple_of(n * v_rows, v_rows), v_rows)
        return pltpu.make_async_copy(v_hbm.at[at, :], vs.at[at, :], loc_v.at[n])

    for n in range(v_parts):
        load_v(n).start()

    barrier = pltpu.get_barrier_semaphore()

    def group_peer(d):
        other = lax.rem(grp + d, groups)
        return other, here(d_z=other // ys, d_y=other % ys)

    def col_peer(d):
        other = lax.rem(col + d, cols)
        return other, here(d_col=other)

    for d in range(1, groups):
        pl.semaphore_signal(barrier, inc=1, device_id=group_peer(d)[1], device_id_type=MESH)
    for d in range(1, cols):
        pl.semaphore_signal(barrier, inc=1, device_id=col_peer(d)[1], device_id_type=MESH)

    load_a.wait()
    rows = a_own.shape[0]
    to = lax.broadcasted_iota(jnp.int32, (rows, rows), 0)
    come = lax.broadcasted_iota(jnp.int32, (rows, rows), 1)
    t_chunk, t_k, t_j = to // mine, (to % mine) // CHUNK, to % CHUNK
    pick = jnp.where(come == t_k * occ + t_chunk * CHUNK + t_j, 1.0, 0.0).astype(bf16)
    own_rows = pl.ds(pl.multiple_of(grp * mine, mine), mine)
    step = 512
    for n in range(depth // step):
        lanes = slice(n * step, (n + 1) * step)
        moved = jnp.dot(pick, a_own[:, lanes], preferred_element_type=f32).astype(bf16)
        for q in range(chunks):
            ab[q, own_rows, lanes] = moved[q * mine : (q + 1) * mine]

    pl.semaphore_wait(barrier, groups - 1 + cols - 1)

    def send_xg(d):
        other, device = group_peer(d)
        return pltpu.make_async_remote_copy(
            src_ref=x_hbm.at[:, pl.ds(pl.multiple_of(other * a_count, a_count), a_count), :],
            dst_ref=x_all.at[col, :, :, pl.ds(pl.multiple_of(grp * x_lanes, x_lanes), x_lanes)],
            send_sem=ss_xg.at[d - 1],
            recv_sem=rs_xg.at[d - 1],
            device_id=device,
            device_id_type=MESH,
        )

    def send_wg(d):
        other, device = group_peer(d)
        return pltpu.make_async_remote_copy(
            src_ref=w_split.at[:, :, pl.ds(pl.multiple_of(other * a_count, a_count), a_count), :],
            dst_ref=w_mid.at[:, :, :, pl.ds(pl.multiple_of(grp * vir, vir), vir)],
            send_sem=ss_wg.at[d - 1],
            recv_sem=rs_wg.at[d - 1],
            device_id=device,
            device_id_type=MESH,
        )

    def amp(q, zz, yy, send, device):
        at = ab.at[q, pl.ds(pl.multiple_of((zz * ys + yy) * mine, mine), mine), :]
        return pltpu.make_async_remote_copy(
            src_ref=at,
            dst_ref=at,
            send_sem=send,
            recv_sem=rs_amp.at[q, zz * ys + yy],
            device_id=device,
            device_id_type=MESH,
        )

    def amp_up(q, zz):
        return amp(q, zz, y, ss_up.at[q, zz], here(d_z=lax.rem(z + 1, zs)))

    def amp_down(q, zz):
        return amp(q, zz, y, ss_down.at[q, zz], here(d_z=lax.rem(z + zs - 1, zs)))

    def amp_row(q, zz):
        return amp(q, zz, y, ss_row.at[q, zz], row_peer)

    def amp_wait(q, zz, yy):
        amp(q, zz, yy, ss_row.at[q, zz], row_peer).wait_recv()

    for d in range(1, groups):
        send_xg(d).start()

    @pl.loop(0, chunks)
    def _(q):
        @pl.when(z < zs - 1)
        def _():
            amp_up(q, z).start()

        @pl.when(z > 0)
        def _():
            amp_down(q, z).start()

        amp_row(q, z).start()

    load_w.wait()
    w_lanes = w_own.shape[2]
    come = lax.broadcasted_iota(jnp.int32, (w_lanes, w_lanes), 0)
    to = lax.broadcasted_iota(jnp.int32, (w_lanes, w_lanes), 1)
    t_owner, t_k, t_c = to // vir, (to % vir) // c_count, to % c_count
    pick = jnp.where(come == t_k * vir + t_owner * c_count + t_c, 1.0, 0.0).astype(bf16)

    @pl.loop(0, i_count // 2)
    def _(n):
        both = w_own[pl.ds(n * 2, 2)].reshape(2 * vir, w_lanes)
        moved = jnp.dot(both, pick, preferred_element_type=f32).astype(bf16)
        for q in range(cols):
            w_split[q, pl.ds(n * 2, 2)] = moved[:, q * vir : (q + 1) * vir].reshape(2, vir, vir)

    for d in range(1, groups):
        send_wg(d).start()
    own_w = pltpu.make_async_copy(
        w_split.at[:, :, pl.ds(pl.multiple_of(grp * a_count, a_count), a_count), :],
        w_mid.at[:, :, :, pl.ds(pl.multiple_of(grp * vir, vir), vir)],
        loc.at[3],
    )
    own_w.start()

    tiles = v_rows // edge

    @pl.loop(0, v_parts)
    def _(n):
        load_v(n).wait()

        @pl.loop(0, tiles)
        def _(m):
            k = n * tiles + m
            at = pl.ds(pl.multiple_of(k * edge, edge), edge)
            for b in range(width // edge):
                lanes = slice(b * edge, (b + 1) * edge)
                live = jnp.full((edge, edge), live_ref[k, b].astype(f32), f32).astype(bf16)
                vs[at, lanes] = vs[at, lanes] * live

    own_x.wait()
    for d in range(1, groups):
        send_xg(d).wait_recv()

    def send_xc(which, slot, device):
        return pltpu.make_async_remote_copy(
            src_ref=x_all.at[which],
            dst_ref=x_all.at[which],
            send_sem=ss_xc.at[slot],
            recv_sem=rs_xc.at[slot],
            device_id=device,
            device_id_type=MESH,
        )

    other_col = lax.rem(col + 2, cols)
    send_xc(col, 0, across).start()
    send_xc(col, 1, sibling).start()

    def forward(q):
        for d in range(1, zs):
            @pl.when(z - d >= 0)
            def _():
                amp_wait(q, z - d, y)

                @pl.when(z < zs - 1)
                def _():
                    amp_up(q, z - d).start()

                amp_row(q, z - d).start()

            @pl.when(z + d < zs)
            def _():
                amp_wait(q, z + d, y)

                @pl.when(z > 0)
                def _():
                    amp_down(q, z + d).start()

                amp_row(q, z + d).start()

    forward(0)

    own_w.wait()
    for d in range(1, groups):
        send_wg(d).wait_recv()

    def send_wc(d):
        other, device = col_peer(d)
        return pltpu.make_async_remote_copy(
            src_ref=w_mid.at[other],
            dst_ref=w_all.at[col],
            send_sem=ss_wc.at[d - 1],
            recv_sem=rs_wc.at[d - 1],
            device_id=device,
            device_id_type=MESH,
        )

    for d in range(1, cols):
        send_wc(d).start()
    w_all[col] = w_mid[col]

    forward(1)

    send_core = lambda q: pltpu.make_async_remote_copy(
        src_ref=part.at[q % 2, :, 1 - core],
        dst_ref=got_core.at[q],
        send_sem=ss_core.at[q],
        recv_sem=rs_core.at[q],
        device_id=sibling,
        device_id_type=MESH,
    )
    send_far = lambda q: pltpu.make_async_remote_copy(
        src_ref=send_x.at[q % 2],
        dst_ref=got_x.at[q],
        send_sem=ss_far.at[q],
        recv_sem=rs_far.at[q],
        device_id=across,
        device_id_type=MESH,
    )

    own_lane = lax.broadcasted_iota(jnp.int32, (occ * a_count, vir), 1) // c_count == col

    def finish(q):
        send_far(q).wait_recv()
        slot = q % 2
        sub = lax.broadcasted_iota(jnp.int32, (CHUNK, vir), 0)
        occ_j = jnp.zeros((CHUNK, vir), f32)
        for j in range(CHUNK):
            occ_j = jnp.where(sub == j, occ_ref[q * CHUNK + j], occ_j)
        at = pl.ds(pl.multiple_of(q * CHUNK, CHUNK), CHUNK)

        @pl.loop(0, a_count)
        def _(a):
            summed = part[slot, far, core, a] + got_core[q, far, a] + got_x[q, a]
            base = vir_ref[grp * a_count + a] + row_ref[...]
            lanes = pl.ds(pl.multiple_of(a * vir, vir), vir)
            for i in range(i_count):
                denom = base - occ_ref[col * i_count + i] - occ_j
                total[i, at, lanes] = summed[i * CHUNK : (i + 1) * CHUNK] / denom

    @pl.loop(0, chunks)
    def _(q):
        slot = q % 2
        for zz in range(zs):
            amp_wait(q, zz, 1 - y)

        @pl.when(q >= 2)
        def _():
            send_core(q - 2).wait_send()

        @pl.loop(0, width // (2 * vir))
        def _(n):
            lanes = pl.ds(pl.multiple_of(n * 2 * vir, 2 * vir), 2 * vir)
            prod = jnp.dot(ab[q], vs[:, lanes], preferred_element_type=f32)
            for o in range(cols):
                for b in range(2):
                    part[slot, o // 2, o % 2, n * 2 + b] = prod[o * quarter : (o + 1) * quarter, b * vir : (b + 1) * vir]

        @pl.loop(0, groups)
        def _(g):
            at = pl.ds(pl.multiple_of(g * mine, mine), mine)
            for c in range(c_count):
                block = ab[q, at, c * vir : (c + 1) * vir].astype(f32)
                for k in range(per_dev):
                    turn[k, pl.ds(c, CHUNK, stride=c_count), :] = block[k * CHUNK : (k + 1) * CHUNK]
            for k in range(per_dev):
                kk = g * per_dev + k
                for j in range(CHUNK):
                    block = turn[k, j * c_count : (j + 1) * c_count, :].astype(bf16)
                    rhs_one[pl.ds(pl.multiple_of(kk * c_count, c_count), c_count), j * vir : (j + 1) * vir] = block
                    rhs_two[j * c_count : (j + 1) * c_count, pl.ds(pl.multiple_of(kk * vir, vir), vir)] = block

        @pl.when(q == 0)
        def _():
            send_xc(other_col, 0, across).wait_recv()
            send_xc(other_col, 2, sibling).start()
            send_xc(col, 1, sibling).wait_recv()
            send_xc(col, 2, sibling).wait_recv()
            for d in range(1, cols):
                send_wc(d).wait_recv()

        x_rows = i_count * a_count
        for o in range(cols):
            exch[o * x_rows : (o + 1) * x_rows, :] = lax.dot_general(
                x_all[o].reshape(x_rows, occ * vir), rhs_two[...], (((1,), (1,)), ((), ())), preferred_element_type=f32
            )
        w_full = w_all[...].reshape(occ * a_count, occ * c_count)
        per_tile = vir // c_count
        for t in range(CHUNK // 2):
            prod = jnp.dot(w_full, rhs_one[:, t * 2 * vir : (t + 1) * 2 * vir], preferred_element_type=f32)
            for jj in range(2):
                j = 2 * t + jj
                tile = exch[:, (j // per_tile) * vir : (j // per_tile + 1) * vir]
                shift = lax.rem(col + cols - j % per_tile, cols) * c_count
                tile = pltpu.roll(tile, shift, 1)
                cyc[jj] = prod[:, jj * vir : (jj + 1) * vir] + jnp.where(own_lane, tile, 0.0)

            @pl.loop(0, a_count)
            def _(a):
                for jj in range(2):
                    at = pl.ds(2 * t + jj, i_count, stride=CHUNK)
                    for o in range(cols):
                        part[slot, o // 2, o % 2, a, at, :] = (
                            part[slot, o // 2, o % 2, a, at, :]
                            + cyc[jj, pl.ds(o * x_rows + a, i_count, stride=a_count), :]
                        )

        send_core(q).start()

        @pl.when(q + 2 < chunks)
        def _():
            forward(q + 2)

        @pl.when(q >= 1)
        def _():
            finish(q - 1)

        send_core(q).wait_recv()

        @pl.when(q >= 2)
        def _():
            send_far(q - 2).wait_send()

        @pl.loop(0, a_count)
        def _(a):
            send_x[slot, a] = part[slot, 1 - far, core, a] + got_core[q, 1 - far, a]

        send_far(q).start()

    finish(chunks - 1)

    @pl.loop(0, i_count)
    def _(i):
        out_ref[pl.ds(pl.multiple_of(i * occ, occ), occ), :] = total[i].astype(bf16)

    for d in range(1, groups):
        send_xg(d).wait_send()
        send_wg(d).wait_send()
    for d in range(1, cols):
        send_wc(d).wait_send()
    for slot in range(3):
        send_xc(col, slot, sibling).wait_send()

    @pl.loop(0, chunks)
    def _(q):
        for zz in range(zs):
            amp_row(q, zz).wait_send()

            @pl.when(jnp.logical_and(z < zs - 1, zz <= z))
            def _():
                amp_up(q, zz).wait_send()

            @pl.when(jnp.logical_and(z > 0, zz >= z))
            def _():
                amp_down(q, zz).wait_send()

    for q in range(chunks - 2, chunks):
        send_core(q).wait_send()
        send_far(q).wait_send()


def fused(amplitudes, ladder_ints, tile_live, cycle_direct, cycle_exchange, eps_occ, eps_vir):
    zs, ys, cols = lax.axis_size("grp"), lax.axis_size("row"), lax.axis_size("col")
    groups = zs * ys
    occ, vir = eps_occ.shape[0], eps_vir.shape[0]
    per_dev, i_count = occ // groups, occ // cols
    a_count, c_count = vir // groups, vir // cols
    depth, width = ladder_ints.shape
    chunks = occ // CHUNK
    mine = per_dev * CHUNK
    all_rows = groups * mine
    quarter = all_rows // cols
    f32, bf16 = jnp.float32, jnp.bfloat16
    dma = pltpu.SemaphoreType.DMA
    any_spec = pl.BlockSpec(memory_space=pl.ANY)
    smem = pl.BlockSpec(memory_space=pltpu.SMEM)
    vmem = pl.BlockSpec(memory_space=pltpu.VMEM)
    v_parts = 8
    return pl.pallas_call(
        fused_kernel,
        out_shape=jax.ShapeDtypeStruct((i_count * occ, width), bf16),
        in_specs=[smem, smem, smem, vmem, any_spec, any_spec, any_spec, any_spec],
        out_specs=vmem,
        scratch_shapes=[
            pltpu.VMEM((depth, width), bf16),
            pltpu.VMEM((chunks, all_rows, depth), bf16),
            pltpu.VMEM((per_dev * occ, depth), bf16),
            pltpu.VMEM((i_count, vir, per_dev * vir), bf16),
            pltpu.VMEM((cols, i_count, vir, vir), bf16),
            pltpu.VMEM((cols, i_count, a_count, groups * vir), bf16),
            pltpu.VMEM((cols, i_count, a_count, groups * vir), bf16),
            pltpu.VMEM((cols, i_count, a_count, occ * vir), bf16),
            pltpu.VMEM((occ * c_count, CHUNK * vir), bf16),
            pltpu.VMEM((CHUNK * c_count, occ * vir), bf16),
            pltpu.VMEM((per_dev, CHUNK * c_count, vir), f32),
            pltpu.VMEM((2, cols // 2, 2, a_count, quarter, vir), f32),
            pltpu.VMEM((2, occ * a_count, vir), f32),
            pltpu.VMEM((occ * a_count, CHUNK * c_count), f32),
            pltpu.VMEM((chunks, cols // 2, a_count, quarter, vir), f32),
            pltpu.VMEM((chunks, a_count, quarter, vir), f32),
            pltpu.VMEM((2, a_count, quarter, vir), f32),
            pltpu.VMEM((i_count, occ, width), f32),
            dma((4,)),
            dma((v_parts,)),
            dma((chunks, zs)),
            dma((chunks, zs)),
            dma((chunks, zs)),
            dma((chunks, groups)),
            dma((groups - 1,)),
            dma((groups - 1,)),
            dma((groups - 1,)),
            dma((groups - 1,)),
            dma((3,)),
            dma((3,)),
            dma((cols - 1,)),
            dma((cols - 1,)),
            dma((chunks,)),
            dma((chunks,)),
            dma((chunks,)),
            dma((chunks,)),
        ],
        compiler_params=pltpu.CompilerParams(collective_id=0, has_side_effects=True, vmem_limit_bytes=LIMIT),
    )(
        tile_live,
        eps_occ,
        eps_vir,
        eps_vir.reshape(1, vir),
        amplitudes,
        ladder_ints,
        cycle_direct.reshape(i_count, vir, per_dev * vir),
        cycle_exchange.reshape(i_count, vir, per_dev * vir),
    )


def cycle_kernel(t_ref, w_ref, x_ref, o_ref):
    occ, step, part, vir = t_ref.shape
    col = lax.axis_index("col")
    rows = w_ref.shape[0]
    u_one = jnp.concatenate(
        [t_ref[:, j].reshape(occ * part, vir) for j in range(step)], axis=1
    )
    direct = jnp.dot(w_ref[...], u_one, preferred_element_type=jnp.float32)
    u_two = jnp.concatenate(
        [t_ref[k].reshape(step * part, vir) for k in range(occ)], axis=1
    )
    exchange = lax.dot_general(
        x_ref[...], u_two, (((1,), (1,)), ((), ())), preferred_element_type=jnp.float32
    )
    own = lax.broadcasted_iota(jnp.int32, (rows, vir), 1) // part == col
    for j in range(step):
        piece = exchange[:, j * part : (j + 1) * part]
        piece = jnp.concatenate([piece] * (vir // part), axis=1)
        o_ref[j] = direct[:, j * vir : (j + 1) * vir] + jnp.where(own, piece, 0.0)


def cycle_sum(four, w, x):
    occ, _, part, vir = four.shape
    rows = w.shape[0]
    step = 8
    return pl.pallas_call(
        cycle_kernel,
        grid=(occ // step,),
        out_shape=jax.ShapeDtypeStruct((occ, rows, vir), jnp.float32),
        in_specs=[
            pl.BlockSpec((occ, step, part, vir), lambda n: (0, n, 0, 0)),
            pl.BlockSpec(w.shape, lambda n: (0, 0)),
            pl.BlockSpec(x.shape, lambda n: (0, 0)),
        ],
        out_specs=pl.BlockSpec((step, rows, vir), lambda n: (n, 0, 0)),
        compiler_params=pltpu.CompilerParams(vmem_limit_bytes=LIMIT),
    )(four, w, x)


def ladder_kernel(live_ref, a_ref, v_ref, o_ref, held):
    edge = v_ref.shape[0] // live_ref.shape[0]
    across = v_ref.shape[1] // edge
    n = pl.program_id(0)

    @pl.when(pl.program_id(1) == 0)
    def _():
        @pl.loop(0, live_ref.shape[0])
        def _(k):
            at = pl.ds(pl.multiple_of(k * edge, edge), edge)
            for b in range(across):
                lanes = slice(b * edge, (b + 1) * edge)
                live = live_ref[k, n * across + b].astype(jnp.float32)
                held[at, lanes] = (v_ref[at, lanes].astype(jnp.float32) * live).astype(jnp.bfloat16)

    o_ref[...] = jnp.dot(a_ref[...], held[...], preferred_element_type=jnp.float32)


def ladder_sum(amps, ints, live):
    rows, depth = amps.shape
    width = ints.shape[1]
    tall = 256
    wide = min(512, width)
    return pl.pallas_call(
        ladder_kernel,
        grid=(width // wide, rows // tall),
        out_shape=jax.ShapeDtypeStruct((rows, width), jnp.float32),
        in_specs=[
            pl.BlockSpec(memory_space=pltpu.SMEM),
            pl.BlockSpec((tall, depth), lambda n, m: (m, 0)),
            pl.BlockSpec((depth, wide), lambda n, m: (0, n)),
        ],
        out_specs=pl.BlockSpec((tall, wide), lambda n, m: (m, n)),
        scratch_shapes=[pltpu.VMEM((depth, wide), jnp.bfloat16)],
        compiler_params=pltpu.CompilerParams(vmem_limit_bytes=LIMIT),
    )(live, amps, ints)


def body(amplitudes, ladder_ints, tile_live, cycle_direct, cycle_exchange, eps_occ, eps_vir):
    groups = lax.axis_size(("grp", "row"))
    columns = lax.axis_size("col")
    col = lax.axis_index("col")
    grp = lax.axis_index(("grp", "row"))
    occ = eps_occ.shape[0]
    vir = eps_vir.shape[0]
    per_dev = occ // groups
    i_count = occ // columns
    a_count = vir // groups
    c_count = vir // columns
    f32 = jnp.float32

    x = cycle_exchange.reshape(i_count, groups, a_count, per_dev * vir)
    x = lax.all_to_all(x, ("grp", "row"), split_axis=1, concat_axis=3, tiled=True)
    x = lax.all_gather(x.reshape(i_count * a_count, occ * vir), "col", axis=0, tiled=True)

    w = cycle_direct.reshape(i_count, groups, a_count, per_dev, columns, c_count)
    w = w.transpose(1, 4, 0, 2, 3, 5).reshape(groups * columns, i_count * a_count, per_dev * c_count)
    w = lax.all_to_all(w, ("grp", "row", "col"), split_axis=0, concat_axis=0, tiled=True)
    w = w.reshape(groups, columns * i_count * a_count, per_dev * c_count)
    w = w.transpose(1, 0, 2).reshape(occ * a_count, occ * c_count)

    amps = lax.all_gather(amplitudes, ("grp", "row"), axis=0, tiled=True)
    ladder = ladder_sum(amps, ladder_ints, tile_live)
    amps, ladder = lax.optimization_barrier((amps, ladder))
    cycle = cycle_sum(amps.reshape(occ, occ, c_count, vir), w, x)
    cycle = cycle.reshape(occ, occ, a_count, vir).transpose(1, 0, 2, 3).reshape(occ * occ, a_count * vir)
    total = lax.psum_scatter(ladder + cycle, "col", scatter_dimension=0, tiled=True)

    occ_local = lax.dynamic_slice_in_dim(eps_occ, col * i_count, i_count)
    vir_local = lax.dynamic_slice_in_dim(eps_vir, grp * a_count, a_count)
    denom = (
        vir_local[None, None, :, None]
        + eps_vir[None, None, None, :]
        - occ_local[:, None, None, None]
        - eps_occ[None, :, None, None]
    ).reshape(i_count * occ, a_count * vir)
    return (total / denom).astype(jnp.bfloat16)


def solution(mesh):
    placed = (
        P(("grp", "row"), "col"),
        P("col", ("grp", "row")),
        P("col", ("grp", "row")),
        P("col", ("grp", "row")),
        P("col", ("grp", "row")),
        P(),
        P(),
    )
    fits = mesh.shape["row"] == 2 and mesh.shape["col"] == 4
    return jax.shard_map(
        fused if fits else body, mesh=mesh, in_specs=placed, out_specs=P("col", ("grp", "row")), check_vma=False
    )
```

```python
import functools

import jax
import jax.numpy as jnp
from jax import lax
from jax.experimental import pallas as pl
from jax.experimental.pallas import tpu as pltpu
from jax.sharding import PartitionSpec as P

LIMIT = 56 * 1024 * 1024
MESH = pl.DeviceIdType.MESH
CHUNK = 4


def ladder_step(a_ref, v_ref, part_ref, per_dev):
    cols, cores, _, quarter, vir = part_ref.shape
    mine = per_dev * CHUNK
    i_count = quarter // CHUNK

    prod = jnp.dot(a_ref[...], v_ref[...], preferred_element_type=jnp.float32)
    for o in range(cols * cores):
        for b in range(v_ref.shape[1] // vir):
            for h in range(i_count // per_dev):
                for j in range(CHUNK):
                    come = o * quarter + h * mine + j * per_dev
                    to = j * i_count + h * per_dev
                    part_ref[o // cores, o % cores, b, to : to + per_dev, :] = prod[
                        come : come + per_dev, b * vir : (b + 1) * vir
                    ]


def turn_step(a_ref, turn, rhs_one, rhs_two, per_dev):
    vir = turn.shape[2]
    mine = per_dev * CHUNK
    c_count = a_ref.shape[1] // vir
    both = turn.shape[0]

    @pl.loop(0, a_ref.shape[0] // mine // both)
    def _(n):
        for h in range(both):
            at = pl.ds(pl.multiple_of((n * both + h) * mine, mine), mine)
            for c in range(c_count):
                block = a_ref[at, c * vir : (c + 1) * vir].astype(jnp.float32)
                for r in range(0, mine, 8):
                    turn[h, c * mine + r : c * mine + r + 8, :] = block[r : r + 8]
            for k in range(per_dev):
                kk = (n * both + h) * per_dev + k
                for j in range(CHUNK):
                    block = turn[h, pl.ds(j * per_dev + k, c_count, stride=mine), :].astype(jnp.bfloat16)
                    rhs_one[pl.ds(pl.multiple_of(kk * c_count, c_count), c_count), j * vir : (j + 1) * vir] = block
                    rhs_two[j * c_count : (j + 1) * c_count, pl.ds(pl.multiple_of(kk * vir, vir), vir)] = block


def cycle_step(w_all, x_all, rhs_one, rhs_two, exch, cyc, part_ref, col):
    cols, i_count, a_count, _ = x_all.shape
    cores = part_ref.shape[1]
    vir = part_ref.shape[4]
    c_count = vir // cols
    x_rows = i_count * a_count
    for o in range(cols):
        exch[o * x_rows : (o + 1) * x_rows, :] = lax.dot_general(
            x_all[o].reshape(x_rows, x_all.shape[3]), rhs_two[...], (((1,), (1,)), ((), ())),
            preferred_element_type=jnp.float32,
        )
    w_full = w_all[...].reshape(cols * x_rows, w_all.shape[3])
    own_lane = lax.broadcasted_iota(jnp.int32, (cols * x_rows, vir), 1) // c_count == col
    prod = jnp.dot(w_full, rhs_one[...], preferred_element_type=jnp.float32)
    gap = a_count + 8
    for j in range(CHUNK):
        tile = exch[:, (j // cols) * vir : (j // cols + 1) * vir]
        shift = lax.rem(col + cols - j % cols, cols) * c_count
        tile = pltpu.roll(tile, shift, 1)
        full = prod[:, j * vir : (j + 1) * vir] + jnp.where(own_lane, tile, 0.0)
        for i in range(cols * i_count):
            cyc[j, i * gap : i * gap + a_count, :] = full[i * a_count : (i + 1) * a_count]
    for a in range(a_count):
        for j in range(CHUNK):
            at = slice(j * i_count, (j + 1) * i_count)
            for o in range(cols):
                part_ref[o // cores, o % cores, a, at, :] = (
                    part_ref[o // cores, o % cores, a, at, :]
                    + cyc[j, pl.ds(o * i_count * gap + a, i_count, stride=gap), :]
                )


def fused_kernel(
    live_ref, occ_ref, vir_ref, row_ref, a_hbm, v_hbm, w_hbm, x_hbm, out_ref,
    vs, ab, a_own, w_own, w_split, w_mid, w_all, x_all, rhs_one, rhs_two, turn, part, cyc, exch, got_core, got_x, send_x, total,
    loc, loc_v, ss_up, ss_down, ss_row, rs_amp, ss_xg, rs_xg, ss_wg, rs_wg, ss_xc, rs_xc, ss_wc, rs_wc,
    ss_core, rs_core, ss_far, rs_far,
):
    f32, bf16 = jnp.float32, jnp.bfloat16
    depth, width = vs.shape
    zs, ys = lax.axis_size("grp"), lax.axis_size("row")
    cols = lax.axis_size("col")
    groups = zs * ys
    z, y, col = lax.axis_index("grp"), lax.axis_index("row"), lax.axis_index("col")
    grp = z * ys + y
    core, far = col % 2, col // 2
    vir = row_ref.shape[1]
    occ = occ_ref.shape[0]
    c_count = depth // vir
    a_count = width // vir
    chunks, all_rows = ab.shape[0], ab.shape[1]
    mine = all_rows // groups
    per_dev = mine // CHUNK
    i_count = occ // cols
    quarter = all_rows // cols
    edge = depth // live_ref.shape[0]

    def here(d_z=None, d_y=None, d_col=None):
        return (z if d_z is None else d_z, y if d_y is None else d_y, col if d_col is None else d_col)

    sibling = here(d_col=col + 1 - 2 * core)
    across = here(d_col=lax.rem(col + 2, cols))
    row_peer = here(d_y=1 - y)

    load_a = pltpu.make_async_copy(a_hbm, a_own, loc.at[0])
    load_a.start()
    load_w = pltpu.make_async_copy(w_hbm, w_own, loc.at[1])
    load_w.start()
    x_lanes = per_dev * vir
    own_x = pltpu.make_async_copy(
        x_hbm.at[:, pl.ds(pl.multiple_of(grp * a_count, a_count), a_count), :],
        x_all.at[col, :, :, pl.ds(pl.multiple_of(grp * x_lanes, x_lanes), x_lanes)],
        loc.at[2],
    )
    own_x.start()
    v_parts = loc_v.shape[0]
    v_rows = depth // v_parts

    def load_v(n):
        at = pl.ds(pl.multiple_of(n * v_rows, v_rows), v_rows)
        return pltpu.make_async_copy(v_hbm.at[at, :], vs.at[at, :], loc_v.at[n])

    for n in range(v_parts):
        load_v(n).start()

    barrier = pltpu.get_barrier_semaphore()

    def group_peer(d):
        other = lax.rem(grp + d, groups)
        return other, here(d_z=other // ys, d_y=other % ys)

    def col_peer(d):
        other = lax.rem(col + d, cols)
        return other, here(d_col=other)

    for d in range(1, groups):
        pl.semaphore_signal(barrier, inc=1, device_id=group_peer(d)[1], device_id_type=MESH)
    for d in range(1, cols):
        pl.semaphore_signal(barrier, inc=1, device_id=col_peer(d)[1], device_id_type=MESH)

    pl.semaphore_wait(barrier, groups - 1 + cols - 1)

    def send_xg(d):
        other, device = group_peer(d)
        return pltpu.make_async_remote_copy(
            src_ref=x_hbm.at[:, pl.ds(pl.multiple_of(other * a_count, a_count), a_count), :],
            dst_ref=x_all.at[col, :, :, pl.ds(pl.multiple_of(grp * x_lanes, x_lanes), x_lanes)],
            send_sem=ss_xg.at[d - 1],
            recv_sem=rs_xg.at[d - 1],
            device_id=device,
            device_id_type=MESH,
        )

    def send_wg(d):
        other, device = group_peer(d)
        return pltpu.make_async_remote_copy(
            src_ref=w_split.at[:, :, pl.ds(pl.multiple_of(other * a_count, a_count), a_count), :],
            dst_ref=w_mid.at[:, :, :, pl.ds(pl.multiple_of(grp * vir, vir), vir)],
            send_sem=ss_wg.at[d - 1],
            recv_sem=rs_wg.at[d - 1],
            device_id=device,
            device_id_type=MESH,
        )

    def amp(q, zz, yy, send, device):
        at = ab.at[q, pl.ds(pl.multiple_of((zz * ys + yy) * mine, mine), mine), :]
        return pltpu.make_async_remote_copy(
            src_ref=at,
            dst_ref=at,
            send_sem=send,
            recv_sem=rs_amp.at[q, zz * ys + yy],
            device_id=device,
            device_id_type=MESH,
        )

    def amp_up(q, zz):
        return amp(q, zz, y, ss_up.at[q, zz], here(d_z=lax.rem(z + 1, zs)))

    def amp_down(q, zz):
        return amp(q, zz, y, ss_down.at[q, zz], here(d_z=lax.rem(z + zs - 1, zs)))

    def amp_row(q, zz):
        return amp(q, zz, y, ss_row.at[q, zz], row_peer)

    def amp_wait(q, zz, yy):
        amp(q, zz, yy, ss_row.at[q, zz], row_peer).wait_recv()

    for d in range(1, groups):
        send_xg(d).start()

    def own_z(q):
        @pl.when(z < zs - 1)
        def _():
            amp_up(q, z).start()

        @pl.when(z > 0)
        def _():
            amp_down(q, z).start()

    load_w.wait()
    w_lanes = w_own.shape[2]
    come = lax.broadcasted_iota(jnp.int32, (w_lanes, w_lanes), 0)
    to = lax.broadcasted_iota(jnp.int32, (w_lanes, w_lanes), 1)
    t_owner, t_k, t_c = to // vir, (to % vir) // c_count, to % c_count
    pick = jnp.where(come == t_k * vir + t_owner * c_count + t_c, 1.0, 0.0).astype(bf16)

    @pl.loop(0, i_count // 2)
    def _(n):
        both = w_own[pl.ds(n * 2, 2)].reshape(2 * vir, w_lanes)
        moved = jnp.dot(both, pick, preferred_element_type=f32).astype(bf16)
        for q in range(cols):
            w_split[q, pl.ds(n * 2, 2)] = moved[:, q * vir : (q + 1) * vir].reshape(2, vir, vir)

    for d in range(1, groups):
        send_wg(d).start()
    own_w = pltpu.make_async_copy(
        w_split.at[:, :, pl.ds(pl.multiple_of(grp * a_count, a_count), a_count), :],
        w_mid.at[:, :, :, pl.ds(pl.multiple_of(grp * vir, vir), vir)],
        loc.at[3],
    )
    own_w.start()

    load_a.wait()
    rows = a_own.shape[0]
    to = lax.broadcasted_iota(jnp.int32, (rows, rows), 0)
    come = lax.broadcasted_iota(jnp.int32, (rows, rows), 1)
    t_chunk, t_j, t_k = to // mine, (to % mine) // per_dev, to % per_dev
    pick = jnp.where(come == t_k * occ + t_chunk * CHUNK + t_j, 1.0, 0.0).astype(bf16)
    own_rows = pl.ds(pl.multiple_of(grp * mine, mine), mine)
    step = 512
    for n in range(depth // step):
        lanes = slice(n * step, (n + 1) * step)
        moved = jnp.dot(pick, a_own[:, lanes], preferred_element_type=f32).astype(bf16)
        for q in range(chunks):
            ab[q, own_rows, lanes] = moved[q * mine : (q + 1) * mine]

    early = min(zs, chunks)

    @pl.loop(0, early)
    def _(q):
        own_z(q)
        amp_row(q, z).start()

    tiles = v_rows // edge

    @pl.loop(0, v_parts)
    def _(n):
        load_v(n).wait()

        @pl.loop(0, tiles)
        def _(m):
            k = n * tiles + m
            at = pl.ds(pl.multiple_of(k * edge, edge), edge)
            for b in range(width // edge):
                lanes = slice(b * edge, (b + 1) * edge)
                live = jnp.full((edge, edge), live_ref[k, b].astype(f32), f32).astype(bf16)
                vs[at, lanes] = vs[at, lanes] * live

    def forward(q, d):
        @pl.when(z - d >= 0)
        def _():
            amp_wait(q, z - d, y)

            @pl.when(z < zs - 1)
            def _():
                amp_up(q, z - d).start()

            amp_row(q, z - d).start()

        @pl.when(z + d < zs)
        def _():
            amp_wait(q, z + d, y)

            @pl.when(z > 0)
            def _():
                amp_down(q, z + d).start()

            amp_row(q, z + d).start()

    def wave(n):
        for d in range(zs - 1, 0, -1):
            if isinstance(n, int):
                if 0 <= n - d < chunks:
                    forward(n - d, d)
            else:
                @pl.when(n - d < chunks)
                def _():
                    forward(n - d, d)

    def own(n):
        @pl.when(n < chunks)
        def _():
            own_z(n)
            amp_row(n, z).start()

    ahead = zs

    wave(1)
    own(early)

    own_x.wait()
    for d in range(1, groups):
        send_xg(d).wait_recv()

    def send_xc(which, slot, device):
        return pltpu.make_async_remote_copy(
            src_ref=x_all.at[which],
            dst_ref=x_all.at[which],
            send_sem=ss_xc.at[slot],
            recv_sem=rs_xc.at[slot],
            device_id=device,
            device_id_type=MESH,
        )

    other_col = lax.rem(col + 2, cols)
    send_xc(col, 0, across).start()
    send_xc(col, 1, sibling).start()

    wave(2)
    own(early + 1)

    own_w.wait()
    for d in range(1, groups):
        send_wg(d).wait_recv()

    def send_wc(d):
        other, device = col_peer(d)
        return pltpu.make_async_remote_copy(
            src_ref=w_mid.at[other],
            dst_ref=w_all.at[col],
            send_sem=ss_wc.at[d - 1],
            recv_sem=rs_wc.at[d - 1],
            device_id=device,
            device_id_type=MESH,
        )

    for d in range(1, cols):
        send_wc(d).start()
    w_all[col] = w_mid[col]

    for n in range(3, ahead):
        wave(n)
        own(early + n - 1)
    send_xc(other_col, 0, across).wait_recv()
    send_xc(other_col, 2, sibling).start()

    send_core = lambda q: pltpu.make_async_remote_copy(
        src_ref=part.at[q % 2, :, 1 - core],
        dst_ref=got_core.at[q],
        send_sem=ss_core.at[q],
        recv_sem=rs_core.at[q],
        device_id=sibling,
        device_id_type=MESH,
    )
    send_far = lambda q: pltpu.make_async_remote_copy(
        src_ref=send_x.at[q % 2],
        dst_ref=got_x.at[q],
        send_sem=ss_far.at[q],
        recv_sem=rs_far.at[q],
        device_id=across,
        device_id_type=MESH,
    )

    def finish(q):
        send_far(q).wait_recv()
        slot = q % 2
        sub = lax.broadcasted_iota(jnp.int32, (i_count, vir), 0)
        occ_i = jnp.zeros((i_count, vir), f32)
        for i in range(i_count):
            occ_i = jnp.where(sub == i, occ_ref[col * i_count + i], occ_i)

        @pl.loop(0, a_count, step=4)
        def _(a_0):
            for da in range(4):
                a = a_0 + da
                base = vir_ref[grp * a_count + a] + row_ref[...] - occ_i
                for j in range(CHUNK):
                    at = slice(j * i_count, (j + 1) * i_count)
                    summed = part[slot, far, core, a, at, :] + got_core[q, far, a, at, :] + got_x[q, a, at, :]
                    to = pl.ds(pl.multiple_of((q * CHUNK + j) * i_count, i_count), i_count)
                    total[a, to, :] = summed / (base - occ_ref[q * CHUNK + j])

    @pl.loop(0, chunks)
    def _(q):
        slot = q % 2
        for zz in range(zs):
            amp_wait(q, zz, 1 - y)

        @pl.when(q >= 2)
        def _():
            send_core(q - 2).wait_send()

        wave(q + ahead)
        own(early + q + ahead - 1)
        ladder_step(ab.at[q], vs, part.at[slot], per_dev)
        turn_step(ab.at[q], turn, rhs_one, rhs_two, per_dev)

        @pl.when(q == 0)
        def _():
            send_xc(col, 1, sibling).wait_recv()
            send_xc(col, 2, sibling).wait_recv()
            for d in range(1, cols):
                send_wc(d).wait_recv()

        cycle_step(w_all, x_all, rhs_one, rhs_two, exch, cyc, part.at[slot], col)
        send_core(q).start()

        @pl.when(q >= 1)
        def _():
            finish(q - 1)

        send_core(q).wait_recv()

        @pl.when(q >= 2)
        def _():
            send_far(q - 2).wait_send()

        @pl.loop(0, a_count)
        def _(a):
            send_x[slot, a] = part[slot, 1 - far, core, a] + got_core[q, 1 - far, a]

        send_far(q).start()

    finish(chunks - 1)

    for a in range(a_count):
        for i in range(i_count):
            block = total[a, pl.ds(i, occ, stride=i_count), :]
            out_ref[i * occ : (i + 1) * occ, a * vir : (a + 1) * vir] = block.astype(bf16)

    for d in range(1, groups):
        send_xg(d).wait_send()
        send_wg(d).wait_send()
    for d in range(1, cols):
        send_wc(d).wait_send()
    for slot in range(3):
        send_xc(col, slot, sibling).wait_send()

    @pl.loop(0, chunks)
    def _(q):
        for zz in range(zs):
            amp_row(q, zz).wait_send()

            @pl.when(jnp.logical_and(z < zs - 1, zz <= z))
            def _():
                amp_up(q, zz).wait_send()

            @pl.when(jnp.logical_and(z > 0, zz >= z))
            def _():
                amp_down(q, zz).wait_send()

    for q in range(chunks - 2, chunks):
        send_core(q).wait_send()
        send_far(q).wait_send()


def fused(amplitudes, ladder_ints, tile_live, cycle_direct, cycle_exchange, eps_occ, eps_vir):
    zs, ys, cols = lax.axis_size("grp"), lax.axis_size("row"), lax.axis_size("col")
    groups = zs * ys
    occ, vir = eps_occ.shape[0], eps_vir.shape[0]
    per_dev, i_count = occ // groups, occ // cols
    a_count, c_count = vir // groups, vir // cols
    depth, width = ladder_ints.shape
    chunks = occ // CHUNK
    mine = per_dev * CHUNK
    all_rows = groups * mine
    quarter = all_rows // cols
    f32, bf16 = jnp.float32, jnp.bfloat16
    dma = pltpu.SemaphoreType.DMA
    any_spec = pl.BlockSpec(memory_space=pl.ANY)
    smem = pl.BlockSpec(memory_space=pltpu.SMEM)
    vmem = pl.BlockSpec(memory_space=pltpu.VMEM)
    v_parts = 8
    return pl.pallas_call(
        fused_kernel,
        out_shape=jax.ShapeDtypeStruct((i_count * occ, width), bf16),
        in_specs=[smem, smem, smem, vmem, any_spec, any_spec, any_spec, any_spec],
        out_specs=vmem,
        scratch_shapes=[
            pltpu.VMEM((depth, width), bf16),
            pltpu.VMEM((chunks, all_rows, depth), bf16),
            pltpu.VMEM((per_dev * occ, depth), bf16),
            pltpu.VMEM((i_count, vir, per_dev * vir), bf16),
            pltpu.VMEM((cols, i_count, vir, vir), bf16),
            pltpu.VMEM((cols, i_count, a_count, groups * vir), bf16),
            pltpu.VMEM((cols, i_count, a_count, groups * vir), bf16),
            pltpu.VMEM((cols, i_count, a_count, occ * vir), bf16),
            pltpu.VMEM((occ * c_count, CHUNK * vir), bf16),
            pltpu.VMEM((CHUNK * c_count, occ * vir), bf16),
            pltpu.VMEM((2, mine * c_count, vir), f32),
            pltpu.VMEM((2, cols // 2, 2, a_count, quarter, vir), f32),
            pltpu.VMEM((CHUNK, occ * (a_count + 8), vir), f32),
            pltpu.VMEM((occ * a_count, CHUNK * c_count), f32),
            pltpu.VMEM((chunks, cols // 2, a_count, quarter, vir), f32),
            pltpu.VMEM((chunks, a_count, quarter, vir), f32),
            pltpu.VMEM((2, a_count, quarter, vir), f32),
            pltpu.VMEM((a_count, i_count * occ, vir), f32),
            dma((4,)),
            dma((v_parts,)),
            dma((chunks, zs)),
            dma((chunks, zs)),
            dma((chunks, zs)),
            dma((chunks, groups)),
            dma((groups - 1,)),
            dma((groups - 1,)),
            dma((groups - 1,)),
            dma((groups - 1,)),
            dma((3,)),
            dma((3,)),
            dma((cols - 1,)),
            dma((cols - 1,)),
            dma((chunks,)),
            dma((chunks,)),
            dma((chunks,)),
            dma((chunks,)),
        ],
        compiler_params=pltpu.CompilerParams(collective_id=0, has_side_effects=True, vmem_limit_bytes=LIMIT),
    )(
        tile_live,
        eps_occ,
        eps_vir,
        eps_vir.reshape(1, vir),
        amplitudes,
        ladder_ints,
        cycle_direct.reshape(i_count, vir, per_dev * vir),
        cycle_exchange.reshape(i_count, vir, per_dev * vir),
    )


def cycle_kernel(t_ref, w_ref, x_ref, o_ref):
    occ, step, part, vir = t_ref.shape
    col = lax.axis_index("col")
    rows = w_ref.shape[0]
    u_one = jnp.concatenate(
        [t_ref[:, j].reshape(occ * part, vir) for j in range(step)], axis=1
    )
    direct = jnp.dot(w_ref[...], u_one, preferred_element_type=jnp.float32)
    u_two = jnp.concatenate(
        [t_ref[k].reshape(step * part, vir) for k in range(occ)], axis=1
    )
    exchange = lax.dot_general(
        x_ref[...], u_two, (((1,), (1,)), ((), ())), preferred_element_type=jnp.float32
    )
    own = lax.broadcasted_iota(jnp.int32, (rows, vir), 1) // part == col
    for j in range(step):
        piece = exchange[:, j * part : (j + 1) * part]
        piece = jnp.concatenate([piece] * (vir // part), axis=1)
        o_ref[j] = direct[:, j * vir : (j + 1) * vir] + jnp.where(own, piece, 0.0)


def cycle_sum(four, w, x):
    occ, _, part, vir = four.shape
    rows = w.shape[0]
    step = 8
    return pl.pallas_call(
        cycle_kernel,
        grid=(occ // step,),
        out_shape=jax.ShapeDtypeStruct((occ, rows, vir), jnp.float32),
        in_specs=[
            pl.BlockSpec((occ, step, part, vir), lambda n: (0, n, 0, 0)),
            pl.BlockSpec(w.shape, lambda n: (0, 0)),
            pl.BlockSpec(x.shape, lambda n: (0, 0)),
        ],
        out_specs=pl.BlockSpec((step, rows, vir), lambda n: (n, 0, 0)),
        compiler_params=pltpu.CompilerParams(vmem_limit_bytes=LIMIT),
    )(four, w, x)


def ladder_kernel(live_ref, a_ref, v_ref, o_ref, held):
    edge = v_ref.shape[0] // live_ref.shape[0]
    across = v_ref.shape[1] // edge
    n = pl.program_id(0)

    @pl.when(pl.program_id(1) == 0)
    def _():
        @pl.loop(0, live_ref.shape[0])
        def _(k):
            at = pl.ds(pl.multiple_of(k * edge, edge), edge)
            for b in range(across):
                lanes = slice(b * edge, (b + 1) * edge)
                live = live_ref[k, n * across + b].astype(jnp.float32)
                held[at, lanes] = (v_ref[at, lanes].astype(jnp.float32) * live).astype(jnp.bfloat16)

    o_ref[...] = jnp.dot(a_ref[...], held[...], preferred_element_type=jnp.float32)


def ladder_sum(amps, ints, live):
    rows, depth = amps.shape
    width = ints.shape[1]
    tall = 256
    wide = min(512, width)
    return pl.pallas_call(
        ladder_kernel,
        grid=(width // wide, rows // tall),
        out_shape=jax.ShapeDtypeStruct((rows, width), jnp.float32),
        in_specs=[
            pl.BlockSpec(memory_space=pltpu.SMEM),
            pl.BlockSpec((tall, depth), lambda n, m: (m, 0)),
            pl.BlockSpec((depth, wide), lambda n, m: (0, n)),
        ],
        out_specs=pl.BlockSpec((tall, wide), lambda n, m: (m, n)),
        scratch_shapes=[pltpu.VMEM((depth, wide), jnp.bfloat16)],
        compiler_params=pltpu.CompilerParams(vmem_limit_bytes=LIMIT),
    )(live, amps, ints)


def body(amplitudes, ladder_ints, tile_live, cycle_direct, cycle_exchange, eps_occ, eps_vir):
    groups = lax.axis_size(("grp", "row"))
    columns = lax.axis_size("col")
    col = lax.axis_index("col")
    grp = lax.axis_index(("grp", "row"))
    occ = eps_occ.shape[0]
    vir = eps_vir.shape[0]
    per_dev = occ // groups
    i_count = occ // columns
    a_count = vir // groups
    c_count = vir // columns
    f32 = jnp.float32

    x = cycle_exchange.reshape(i_count, groups, a_count, per_dev * vir)
    x = lax.all_to_all(x, ("grp", "row"), split_axis=1, concat_axis=3, tiled=True)
    x = lax.all_gather(x.reshape(i_count * a_count, occ * vir), "col", axis=0, tiled=True)

    w = cycle_direct.reshape(i_count, groups, a_count, per_dev, columns, c_count)
    w = w.transpose(1, 4, 0, 2, 3, 5).reshape(groups * columns, i_count * a_count, per_dev * c_count)
    w = lax.all_to_all(w, ("grp", "row", "col"), split_axis=0, concat_axis=0, tiled=True)
    w = w.reshape(groups, columns * i_count * a_count, per_dev * c_count)
    w = w.transpose(1, 0, 2).reshape(occ * a_count, occ * c_count)

    amps = lax.all_gather(amplitudes, ("grp", "row"), axis=0, tiled=True)
    ladder = ladder_sum(amps, ladder_ints, tile_live)
    amps, ladder = lax.optimization_barrier((amps, ladder))
    cycle = cycle_sum(amps.reshape(occ, occ, c_count, vir), w, x)
    cycle = cycle.reshape(occ, occ, a_count, vir).transpose(1, 0, 2, 3).reshape(occ * occ, a_count * vir)
    total = lax.psum_scatter(ladder + cycle, "col", scatter_dimension=0, tiled=True)

    occ_local = lax.dynamic_slice_in_dim(eps_occ, col * i_count, i_count)
    vir_local = lax.dynamic_slice_in_dim(eps_vir, grp * a_count, a_count)
    denom = (
        vir_local[None, None, :, None]
        + eps_vir[None, None, None, :]
        - occ_local[:, None, None, None]
        - eps_occ[None, :, None, None]
    ).reshape(i_count * occ, a_count * vir)
    return (total / denom).astype(jnp.bfloat16)


def solution(mesh):
    placed = (
        P(("grp", "row"), "col"),
        P("col", ("grp", "row")),
        P("col", ("grp", "row")),
        P("col", ("grp", "row")),
        P("col", ("grp", "row")),
        P(),
        P(),
    )
    fits = mesh.shape["row"] == 2 and mesh.shape["col"] == 4
    return jax.shard_map(
        fused if fits else body, mesh=mesh, in_specs=placed, out_specs=P("col", ("grp", "row")), check_vma=False
    )
```

```python
import functools

import jax
import jax.numpy as jnp
from jax import lax
from jax.experimental import pallas as pl
from jax.experimental.pallas import tpu as pltpu
from jax.sharding import PartitionSpec as P

LIMIT = 56 * 1024 * 1024
MESH = pl.DeviceIdType.MESH
CHUNK = 4


def ladder_step(a_ref, v_ref, part_ref, per_dev):
    cols, cores, _, quarter, vir = part_ref.shape
    mine = per_dev * CHUNK
    i_count = quarter // CHUNK

    prod = jnp.dot(a_ref[...], v_ref[...], preferred_element_type=jnp.float32)
    for o in range(cols * cores):
        for b in range(v_ref.shape[1] // vir):
            for h in range(i_count // per_dev):
                for j in range(CHUNK):
                    come = o * quarter + h * mine + j * per_dev
                    to = j * i_count + h * per_dev
                    part_ref[o // cores, o % cores, b, to : to + per_dev, :] = prod[
                        come : come + per_dev, b * vir : (b + 1) * vir
                    ]


def turn_step(a_ref, turn, rhs_one, rhs_two, per_dev):
    vir = turn.shape[2]
    mine = per_dev * CHUNK
    c_count = a_ref.shape[1] // vir
    both = turn.shape[0]

    @pl.loop(0, a_ref.shape[0] // mine // both)
    def _(n):
        for h in range(both):
            at = pl.ds(pl.multiple_of((n * both + h) * mine, mine), mine)
            for c in range(c_count):
                block = a_ref[at, c * vir : (c + 1) * vir].astype(jnp.float32)
                for r in range(0, mine, 8):
                    turn[h, c * mine + r : c * mine + r + 8, :] = block[r : r + 8]
            for k in range(per_dev):
                kk = (n * both + h) * per_dev + k
                for j in range(CHUNK):
                    block = turn[h, pl.ds(j * per_dev + k, c_count, stride=mine), :].astype(jnp.bfloat16)
                    rhs_one[pl.ds(pl.multiple_of(kk * c_count, c_count), c_count), j * vir : (j + 1) * vir] = block
                    rhs_two[j * c_count : (j + 1) * c_count, pl.ds(pl.multiple_of(kk * vir, vir), vir)] = block


def cycle_step(w_all, x_all, rhs_one, rhs_two, exch, cyc, part_ref, col):
    cols, i_count, a_count, _ = x_all.shape
    cores = part_ref.shape[1]
    vir = part_ref.shape[4]
    c_count = vir // cols
    x_rows = i_count * a_count
    for o in range(cols):
        exch[o * x_rows : (o + 1) * x_rows, :] = lax.dot_general(
            x_all[o].reshape(x_rows, x_all.shape[3]), rhs_two[...], (((1,), (1,)), ((), ())),
            preferred_element_type=jnp.float32,
        )
    w_full = w_all[...].reshape(cols * x_rows, w_all.shape[3])
    own_lane = lax.broadcasted_iota(jnp.int32, (cols * x_rows, vir), 1) // c_count == col
    prod = jnp.dot(w_full, rhs_one[...], preferred_element_type=jnp.float32)
    gap = a_count + 8
    for j in range(CHUNK):
        tile = exch[:, (j // cols) * vir : (j // cols + 1) * vir]
        shift = lax.rem(col + cols - j % cols, cols) * c_count
        tile = pltpu.roll(tile, shift, 1)
        full = prod[:, j * vir : (j + 1) * vir] + jnp.where(own_lane, tile, 0.0)
        for i in range(cols * i_count):
            cyc[j, i * gap : i * gap + a_count, :] = full[i * a_count : (i + 1) * a_count]
    for a in range(a_count):
        for j in range(CHUNK):
            at = slice(j * i_count, (j + 1) * i_count)
            for o in range(cols):
                part_ref[o // cores, o % cores, a, at, :] = (
                    part_ref[o // cores, o % cores, a, at, :]
                    + cyc[j, pl.ds(o * i_count * gap + a, i_count, stride=gap), :]
                )


def fused_kernel(
    live_ref, occ_ref, vir_ref, row_ref, a_hbm, v_hbm, w_hbm, x_hbm, out_ref,
    vs, ab, a_own, w_own, w_split, w_mid, w_all, x_all, rhs_one, rhs_two, turn, part, cyc, exch, got_core, got_x, send_x, total,
    loc, loc_v, ss_up, ss_down, ss_row, rs_amp, ss_xg, rs_xg, ss_wg, rs_wg, ss_xc, rs_xc, ss_wc, rs_wc,
    ss_core, rs_core, ss_far, rs_far,
):
    f32, bf16 = jnp.float32, jnp.bfloat16
    depth, width = vs.shape
    zs, ys = lax.axis_size("grp"), lax.axis_size("row")
    cols = lax.axis_size("col")
    groups = zs * ys
    z, y, col = lax.axis_index("grp"), lax.axis_index("row"), lax.axis_index("col")
    grp = z * ys + y
    core, far = col % 2, col // 2
    vir = row_ref.shape[1]
    occ = occ_ref.shape[0]
    c_count = depth // vir
    a_count = width // vir
    chunks, all_rows = ab.shape[0], ab.shape[1]
    mine = all_rows // groups
    per_dev = mine // CHUNK
    i_count = occ // cols
    quarter = all_rows // cols
    edge = depth // live_ref.shape[0]

    def here(d_z=None, d_y=None, d_col=None):
        return (z if d_z is None else d_z, y if d_y is None else d_y, col if d_col is None else d_col)

    sibling = here(d_col=col + 1 - 2 * core)
    across = here(d_col=lax.rem(col + 2, cols))
    row_peer = here(d_y=1 - y)

    load_a = pltpu.make_async_copy(a_hbm, a_own, loc.at[0])
    load_a.start()
    load_w = pltpu.make_async_copy(w_hbm, w_own, loc.at[1])
    load_w.start()
    x_lanes = per_dev * vir
    own_x = pltpu.make_async_copy(
        x_hbm.at[:, pl.ds(pl.multiple_of(grp * a_count, a_count), a_count), :],
        x_all.at[col, :, :, pl.ds(pl.multiple_of(grp * x_lanes, x_lanes), x_lanes)],
        loc.at[2],
    )
    own_x.start()
    v_parts = loc_v.shape[0]
    v_rows = depth // v_parts

    def load_v(n):
        at = pl.ds(pl.multiple_of(n * v_rows, v_rows), v_rows)
        return pltpu.make_async_copy(v_hbm.at[at, :], vs.at[at, :], loc_v.at[n])

    for n in range(v_parts):
        load_v(n).start()

    barrier = pltpu.get_barrier_semaphore()

    def group_peer(d):
        other = lax.rem(grp + d, groups)
        return other, here(d_z=other // ys, d_y=other % ys)

    def col_peer(d):
        other = lax.rem(col + d, cols)
        return other, here(d_col=other)

    for d in range(1, groups):
        pl.semaphore_signal(barrier, inc=1, device_id=group_peer(d)[1], device_id_type=MESH)
    for d in range(1, cols):
        pl.semaphore_signal(barrier, inc=1, device_id=col_peer(d)[1], device_id_type=MESH)

    pl.semaphore_wait(barrier, groups - 1 + cols - 1)

    def send_xg(d):
        other, device = group_peer(d)
        return pltpu.make_async_remote_copy(
            src_ref=x_hbm.at[:, pl.ds(pl.multiple_of(other * a_count, a_count), a_count), :],
            dst_ref=x_all.at[col, :, :, pl.ds(pl.multiple_of(grp * x_lanes, x_lanes), x_lanes)],
            send_sem=ss_xg.at[d - 1],
            recv_sem=rs_xg.at[d - 1],
            device_id=device,
            device_id_type=MESH,
        )

    def send_wg(d):
        other, device = group_peer(d)
        return pltpu.make_async_remote_copy(
            src_ref=w_split.at[:, :, pl.ds(pl.multiple_of(other * a_count, a_count), a_count), :],
            dst_ref=w_mid.at[:, :, :, pl.ds(pl.multiple_of(grp * vir, vir), vir)],
            send_sem=ss_wg.at[d - 1],
            recv_sem=rs_wg.at[d - 1],
            device_id=device,
            device_id_type=MESH,
        )

    def amp(q, zz, yy, send, device):
        at = ab.at[q, pl.ds(pl.multiple_of((zz * ys + yy) * mine, mine), mine), :]
        return pltpu.make_async_remote_copy(
            src_ref=at,
            dst_ref=at,
            send_sem=send,
            recv_sem=rs_amp.at[q, zz * ys + yy],
            device_id=device,
            device_id_type=MESH,
        )

    def amp_up(q, zz):
        return amp(q, zz, y, ss_up.at[q, zz], here(d_z=lax.rem(z + 1, zs)))

    def amp_down(q, zz):
        return amp(q, zz, y, ss_down.at[q, zz], here(d_z=lax.rem(z + zs - 1, zs)))

    def amp_row(q, zz):
        return amp(q, zz, y, ss_row.at[q, zz], row_peer)

    def amp_wait(q, zz, yy):
        amp(q, zz, yy, ss_row.at[q, zz], row_peer).wait_recv()

    for d in range(1, groups):
        send_xg(d).start()

    def own_z(q):
        @pl.when(z < zs - 1)
        def _():
            amp_up(q, z).start()

        @pl.when(z > 0)
        def _():
            amp_down(q, z).start()

    load_w.wait()
    w_lanes = w_own.shape[2]
    come = lax.broadcasted_iota(jnp.int32, (w_lanes, w_lanes), 0)
    to = lax.broadcasted_iota(jnp.int32, (w_lanes, w_lanes), 1)
    t_owner, t_k, t_c = to // vir, (to % vir) // c_count, to % c_count
    pick = jnp.where(come == t_k * vir + t_owner * c_count + t_c, 1.0, 0.0).astype(bf16)

    @pl.loop(0, i_count // 2)
    def _(n):
        both = w_own[pl.ds(n * 2, 2)].reshape(2 * vir, w_lanes)
        moved = jnp.dot(both, pick, preferred_element_type=f32).astype(bf16)
        for q in range(cols):
            w_split[q, pl.ds(n * 2, 2)] = moved[:, q * vir : (q + 1) * vir].reshape(2, vir, vir)

    own_w = pltpu.make_async_copy(
        w_split.at[:, :, pl.ds(pl.multiple_of(grp * a_count, a_count), a_count), :],
        w_mid.at[:, :, :, pl.ds(pl.multiple_of(grp * vir, vir), vir)],
        loc.at[3],
    )
    own_w.start()

    load_a.wait()
    rows = a_own.shape[0]
    to = lax.broadcasted_iota(jnp.int32, (rows, rows), 0)
    come = lax.broadcasted_iota(jnp.int32, (rows, rows), 1)
    t_chunk, t_j, t_k = to // mine, (to % mine) // per_dev, to % per_dev
    pick = jnp.where(come == t_k * occ + t_chunk * CHUNK + t_j, 1.0, 0.0).astype(bf16)
    own_rows = pl.ds(pl.multiple_of(grp * mine, mine), mine)
    step = 512
    for n in range(depth // step):
        lanes = slice(n * step, (n + 1) * step)
        moved = jnp.dot(pick, a_own[:, lanes], preferred_element_type=f32).astype(bf16)
        for q in range(chunks):
            ab[q, own_rows, lanes] = moved[q * mine : (q + 1) * mine]

    early = min(zs, chunks)

    @pl.loop(0, early)
    def _(q):
        own_z(q)

    @pl.loop(0, chunks)
    def _(q):
        amp_row(q, z).start()

    tiles = v_rows // edge

    @pl.loop(0, v_parts)
    def _(n):
        load_v(n).wait()

        @pl.loop(0, tiles)
        def _(m):
            k = n * tiles + m
            at = pl.ds(pl.multiple_of(k * edge, edge), edge)
            for b in range(width // edge):
                lanes = slice(b * edge, (b + 1) * edge)
                live = jnp.full((edge, edge), live_ref[k, b].astype(f32), f32).astype(bf16)
                vs[at, lanes] = vs[at, lanes] * live

    def forward(q, d):
        @pl.when(z - d >= 0)
        def _():
            amp_wait(q, z - d, y)

            @pl.when(z < zs - 1)
            def _():
                amp_up(q, z - d).start()

            amp_row(q, z - d).start()

        @pl.when(z + d < zs)
        def _():
            amp_wait(q, z + d, y)

            @pl.when(z > 0)
            def _():
                amp_down(q, z + d).start()

            amp_row(q, z + d).start()

    def wave(n):
        hops(n, range(zs - 1, 0, -1))

    def hops(n, which):
        for d in which:
            if isinstance(n, int):
                if 0 <= n - d < chunks:
                    forward(n - d, d)
            else:
                @pl.when(n - d < chunks)
                def _():
                    forward(n - d, d)

    def own(n):
        @pl.when(n < chunks)
        def _():
            own_z(n)

    ahead = zs

    wave(1)
    own(early)

    own_x.wait()
    for d in range(1, groups):
        send_xg(d).wait_recv()

    def send_xc(which, slot, device):
        return pltpu.make_async_remote_copy(
            src_ref=x_all.at[which],
            dst_ref=x_all.at[which],
            send_sem=ss_xc.at[slot],
            recv_sem=rs_xc.at[slot],
            device_id=device,
            device_id_type=MESH,
        )

    other_col = lax.rem(col + 2, cols)
    send_xc(col, 0, across).start()
    send_xc(col, 1, sibling).start()

    for d in range(1, groups):
        send_wg(d).start()
    wave(2)
    own(early + 1)

    own_w.wait()
    for d in range(1, groups):
        send_wg(d).wait_recv()

    def send_wc(d):
        other, device = col_peer(d)
        return pltpu.make_async_remote_copy(
            src_ref=w_mid.at[other],
            dst_ref=w_all.at[col],
            send_sem=ss_wc.at[d - 1],
            recv_sem=rs_wc.at[d - 1],
            device_id=device,
            device_id_type=MESH,
        )

    for d in range(1, cols):
        send_wc(d).start()
    w_all[col] = w_mid[col]

    for n in range(3, ahead):
        wave(n)
        own(early + n - 1)
    send_xc(other_col, 0, across).wait_recv()
    send_xc(other_col, 2, sibling).start()

    send_core = lambda q: pltpu.make_async_remote_copy(
        src_ref=part.at[q % 2, :, 1 - core],
        dst_ref=got_core.at[q],
        send_sem=ss_core.at[q],
        recv_sem=rs_core.at[q],
        device_id=sibling,
        device_id_type=MESH,
    )
    send_far = lambda q: pltpu.make_async_remote_copy(
        src_ref=send_x.at[q % 2],
        dst_ref=got_x.at[q],
        send_sem=ss_far.at[q],
        recv_sem=rs_far.at[q],
        device_id=across,
        device_id_type=MESH,
    )

    def finish(q):
        send_far(q).wait_recv()
        slot = q % 2
        sub = lax.broadcasted_iota(jnp.int32, (i_count, vir), 0)
        occ_i = jnp.zeros((i_count, vir), f32)
        for i in range(i_count):
            occ_i = jnp.where(sub == i, occ_ref[col * i_count + i], occ_i)

        @pl.loop(0, a_count, step=4)
        def _(a_0):
            for da in range(4):
                a = a_0 + da
                base = vir_ref[grp * a_count + a] + row_ref[...] - occ_i
                for j in range(CHUNK):
                    at = slice(j * i_count, (j + 1) * i_count)
                    summed = part[slot, far, core, a, at, :] + got_core[q, far, a, at, :] + got_x[q, a, at, :]
                    to = pl.ds(pl.multiple_of((q * CHUNK + j) * i_count, i_count), i_count)
                    total[a, to, :] = summed / (base - occ_ref[q * CHUNK + j])

    @pl.loop(0, chunks)
    def _(q):
        slot = q % 2
        for zz in range(zs):
            amp_wait(q, zz, 1 - y)

        @pl.when(q >= 2)
        def _():
            send_core(q - 2).wait_send()

        hops(q + ahead, [zs - 1])
        ladder_step(ab.at[q], vs, part.at[slot], per_dev)
        hops(q + ahead, range(zs - 2, 0, -1))
        own(early + q + ahead - 1)
        turn_step(ab.at[q], turn, rhs_one, rhs_two, per_dev)

        @pl.when(q == 0)
        def _():
            send_xc(col, 1, sibling).wait_recv()
            send_xc(col, 2, sibling).wait_recv()
            for d in range(1, cols):
                send_wc(d).wait_recv()

        cycle_step(w_all, x_all, rhs_one, rhs_two, exch, cyc, part.at[slot], col)
        send_core(q).start()

        @pl.when(q >= 1)
        def _():
            finish(q - 1)

        send_core(q).wait_recv()

        @pl.when(q >= 2)
        def _():
            send_far(q - 2).wait_send()

        @pl.loop(0, a_count)
        def _(a):
            send_x[slot, a] = part[slot, 1 - far, core, a] + got_core[q, 1 - far, a]

        send_far(q).start()

    finish(chunks - 1)

    for a in range(a_count):
        for i in range(i_count):
            block = total[a, pl.ds(i, occ, stride=i_count), :]
            out_ref[i * occ : (i + 1) * occ, a * vir : (a + 1) * vir] = block.astype(bf16)

    for d in range(1, groups):
        send_xg(d).wait_send()
        send_wg(d).wait_send()
    for d in range(1, cols):
        send_wc(d).wait_send()
    for slot in range(3):
        send_xc(col, slot, sibling).wait_send()

    @pl.loop(0, chunks)
    def _(q):
        for zz in range(zs):
            amp_row(q, zz).wait_send()

            @pl.when(jnp.logical_and(z < zs - 1, zz <= z))
            def _():
                amp_up(q, zz).wait_send()

            @pl.when(jnp.logical_and(z > 0, zz >= z))
            def _():
                amp_down(q, zz).wait_send()

    for q in range(chunks - 2, chunks):
        send_core(q).wait_send()
        send_far(q).wait_send()


def fused(amplitudes, ladder_ints, tile_live, cycle_direct, cycle_exchange, eps_occ, eps_vir):
    zs, ys, cols = lax.axis_size("grp"), lax.axis_size("row"), lax.axis_size("col")
    groups = zs * ys
    occ, vir = eps_occ.shape[0], eps_vir.shape[0]
    per_dev, i_count = occ // groups, occ // cols
    a_count, c_count = vir // groups, vir // cols
    depth, width = ladder_ints.shape
    chunks = occ // CHUNK
    mine = per_dev * CHUNK
    all_rows = groups * mine
    quarter = all_rows // cols
    f32, bf16 = jnp.float32, jnp.bfloat16
    dma = pltpu.SemaphoreType.DMA
    any_spec = pl.BlockSpec(memory_space=pl.ANY)
    smem = pl.BlockSpec(memory_space=pltpu.SMEM)
    vmem = pl.BlockSpec(memory_space=pltpu.VMEM)
    v_parts = 8
    return pl.pallas_call(
        fused_kernel,
        out_shape=jax.ShapeDtypeStruct((i_count * occ, width), bf16),
        in_specs=[smem, smem, smem, vmem, any_spec, any_spec, any_spec, any_spec],
        out_specs=vmem,
        scratch_shapes=[
            pltpu.VMEM((depth, width), bf16),
            pltpu.VMEM((chunks, all_rows, depth), bf16),
            pltpu.VMEM((per_dev * occ, depth), bf16),
            pltpu.VMEM((i_count, vir, per_dev * vir), bf16),
            pltpu.VMEM((cols, i_count, vir, vir), bf16),
            pltpu.VMEM((cols, i_count, a_count, groups * vir), bf16),
            pltpu.VMEM((cols, i_count, a_count, groups * vir), bf16),
            pltpu.VMEM((cols, i_count, a_count, occ * vir), bf16),
            pltpu.VMEM((occ * c_count, CHUNK * vir), bf16),
            pltpu.VMEM((CHUNK * c_count, occ * vir), bf16),
            pltpu.VMEM((2, mine * c_count, vir), f32),
            pltpu.VMEM((2, cols // 2, 2, a_count, quarter, vir), f32),
            pltpu.VMEM((CHUNK, occ * (a_count + 8), vir), f32),
            pltpu.VMEM((occ * a_count, CHUNK * c_count), f32),
            pltpu.VMEM((chunks, cols // 2, a_count, quarter, vir), f32),
            pltpu.VMEM((chunks, a_count, quarter, vir), f32),
            pltpu.VMEM((2, a_count, quarter, vir), f32),
            pltpu.VMEM((a_count, i_count * occ, vir), f32),
            dma((4,)),
            dma((v_parts,)),
            dma((chunks, zs)),
            dma((chunks, zs)),
            dma((chunks, zs)),
            dma((chunks, groups)),
            dma((groups - 1,)),
            dma((groups - 1,)),
            dma((groups - 1,)),
            dma((groups - 1,)),
            dma((3,)),
            dma((3,)),
            dma((cols - 1,)),
            dma((cols - 1,)),
            dma((chunks,)),
            dma((chunks,)),
            dma((chunks,)),
            dma((chunks,)),
        ],
        compiler_params=pltpu.CompilerParams(collective_id=0, has_side_effects=True, vmem_limit_bytes=LIMIT),
    )(
        tile_live,
        eps_occ,
        eps_vir,
        eps_vir.reshape(1, vir),
        amplitudes,
        ladder_ints,
        cycle_direct.reshape(i_count, vir, per_dev * vir),
        cycle_exchange.reshape(i_count, vir, per_dev * vir),
    )


def cycle_kernel(t_ref, w_ref, x_ref, o_ref):
    occ, step, part, vir = t_ref.shape
    col = lax.axis_index("col")
    rows = w_ref.shape[0]
    u_one = jnp.concatenate(
        [t_ref[:, j].reshape(occ * part, vir) for j in range(step)], axis=1
    )
    direct = jnp.dot(w_ref[...], u_one, preferred_element_type=jnp.float32)
    u_two = jnp.concatenate(
        [t_ref[k].reshape(step * part, vir) for k in range(occ)], axis=1
    )
    exchange = lax.dot_general(
        x_ref[...], u_two, (((1,), (1,)), ((), ())), preferred_element_type=jnp.float32
    )
    own = lax.broadcasted_iota(jnp.int32, (rows, vir), 1) // part == col
    for j in range(step):
        piece = exchange[:, j * part : (j + 1) * part]
        piece = jnp.concatenate([piece] * (vir // part), axis=1)
        o_ref[j] = direct[:, j * vir : (j + 1) * vir] + jnp.where(own, piece, 0.0)


def cycle_sum(four, w, x):
    occ, _, part, vir = four.shape
    rows = w.shape[0]
    step = 8
    return pl.pallas_call(
        cycle_kernel,
        grid=(occ // step,),
        out_shape=jax.ShapeDtypeStruct((occ, rows, vir), jnp.float32),
        in_specs=[
            pl.BlockSpec((occ, step, part, vir), lambda n: (0, n, 0, 0)),
            pl.BlockSpec(w.shape, lambda n: (0, 0)),
            pl.BlockSpec(x.shape, lambda n: (0, 0)),
        ],
        out_specs=pl.BlockSpec((step, rows, vir), lambda n: (n, 0, 0)),
        compiler_params=pltpu.CompilerParams(vmem_limit_bytes=LIMIT),
    )(four, w, x)


def ladder_kernel(live_ref, a_ref, v_ref, o_ref, held):
    edge = v_ref.shape[0] // live_ref.shape[0]
    across = v_ref.shape[1] // edge
    n = pl.program_id(0)

    @pl.when(pl.program_id(1) == 0)
    def _():
        @pl.loop(0, live_ref.shape[0])
        def _(k):
            at = pl.ds(pl.multiple_of(k * edge, edge), edge)
            for b in range(across):
                lanes = slice(b * edge, (b + 1) * edge)
                live = live_ref[k, n * across + b].astype(jnp.float32)
                held[at, lanes] = (v_ref[at, lanes].astype(jnp.float32) * live).astype(jnp.bfloat16)

    o_ref[...] = jnp.dot(a_ref[...], held[...], preferred_element_type=jnp.float32)


def ladder_sum(amps, ints, live):
    rows, depth = amps.shape
    width = ints.shape[1]
    tall = 256
    wide = min(512, width)
    return pl.pallas_call(
        ladder_kernel,
        grid=(width // wide, rows // tall),
        out_shape=jax.ShapeDtypeStruct((rows, width), jnp.float32),
        in_specs=[
            pl.BlockSpec(memory_space=pltpu.SMEM),
            pl.BlockSpec((tall, depth), lambda n, m: (m, 0)),
            pl.BlockSpec((depth, wide), lambda n, m: (0, n)),
        ],
        out_specs=pl.BlockSpec((tall, wide), lambda n, m: (m, n)),
        scratch_shapes=[pltpu.VMEM((depth, wide), jnp.bfloat16)],
        compiler_params=pltpu.CompilerParams(vmem_limit_bytes=LIMIT),
    )(live, amps, ints)


def body(amplitudes, ladder_ints, tile_live, cycle_direct, cycle_exchange, eps_occ, eps_vir):
    groups = lax.axis_size(("grp", "row"))
    columns = lax.axis_size("col")
    col = lax.axis_index("col")
    grp = lax.axis_index(("grp", "row"))
    occ = eps_occ.shape[0]
    vir = eps_vir.shape[0]
    per_dev = occ // groups
    i_count = occ // columns
    a_count = vir // groups
    c_count = vir // columns
    f32 = jnp.float32

    x = cycle_exchange.reshape(i_count, groups, a_count, per_dev * vir)
    x = lax.all_to_all(x, ("grp", "row"), split_axis=1, concat_axis=3, tiled=True)
    x = lax.all_gather(x.reshape(i_count * a_count, occ * vir), "col", axis=0, tiled=True)

    w = cycle_direct.reshape(i_count, groups, a_count, per_dev, columns, c_count)
    w = w.transpose(1, 4, 0, 2, 3, 5).reshape(groups * columns, i_count * a_count, per_dev * c_count)
    w = lax.all_to_all(w, ("grp", "row", "col"), split_axis=0, concat_axis=0, tiled=True)
    w = w.reshape(groups, columns * i_count * a_count, per_dev * c_count)
    w = w.transpose(1, 0, 2).reshape(occ * a_count, occ * c_count)

    amps = lax.all_gather(amplitudes, ("grp", "row"), axis=0, tiled=True)
    ladder = ladder_sum(amps, ladder_ints, tile_live)
    amps, ladder = lax.optimization_barrier((amps, ladder))
    cycle = cycle_sum(amps.reshape(occ, occ, c_count, vir), w, x)
    cycle = cycle.reshape(occ, occ, a_count, vir).transpose(1, 0, 2, 3).reshape(occ * occ, a_count * vir)
    total = lax.psum_scatter(ladder + cycle, "col", scatter_dimension=0, tiled=True)

    occ_local = lax.dynamic_slice_in_dim(eps_occ, col * i_count, i_count)
    vir_local = lax.dynamic_slice_in_dim(eps_vir, grp * a_count, a_count)
    denom = (
        vir_local[None, None, :, None]
        + eps_vir[None, None, None, :]
        - occ_local[:, None, None, None]
        - eps_occ[None, :, None, None]
    ).reshape(i_count * occ, a_count * vir)
    return (total / denom).astype(jnp.bfloat16)


def solution(mesh):
    placed = (
        P(("grp", "row"), "col"),
        P("col", ("grp", "row")),
        P("col", ("grp", "row")),
        P("col", ("grp", "row")),
        P("col", ("grp", "row")),
        P(),
        P(),
    )
    fits = mesh.shape["row"] == 2 and mesh.shape["col"] == 4
    return jax.shard_map(
        fused if fits else body, mesh=mesh, in_specs=placed, out_specs=P("col", ("grp", "row")), check_vma=False
    )
```

```python
import functools

import jax
import jax.numpy as jnp
from jax import lax
from jax.experimental import pallas as pl
from jax.experimental.pallas import tpu as pltpu
from jax.sharding import PartitionSpec as P

LIMIT = 56 * 1024 * 1024
MESH = pl.DeviceIdType.MESH
HALVES = 2
CHUNK = 4


def ladder_step(a_ref, v_ref, part_ref, per_dev):
    cols, cores, _, quarter, vir = part_ref.shape
    mine = per_dev * CHUNK
    i_count = quarter // CHUNK

    prod = jnp.dot(a_ref[...], v_ref[...], preferred_element_type=jnp.float32)
    for o in range(cols * cores):
        for b in range(v_ref.shape[1] // vir):
            for h in range(i_count // per_dev):
                for j in range(CHUNK):
                    come = o * quarter + h * mine + j * per_dev
                    to = j * i_count + h * per_dev
                    part_ref[o // cores, o % cores, b, to : to + per_dev, :] = prod[
                        come : come + per_dev, b * vir : (b + 1) * vir
                    ]


def turn_step(a_ref, turn, rhs_one, rhs_two, per_dev):
    vir = turn.shape[2]
    mine = per_dev * CHUNK
    c_count = a_ref.shape[1] // vir
    both = turn.shape[0]

    @pl.loop(0, a_ref.shape[0] // mine // both)
    def _(n):
        for h in range(both):
            at = pl.ds(pl.multiple_of((n * both + h) * mine, mine), mine)
            for c in range(c_count):
                block = a_ref[at, c * vir : (c + 1) * vir].astype(jnp.float32)
                for r in range(0, mine, 8):
                    turn[h, c * mine + r : c * mine + r + 8, :] = block[r : r + 8]
            for k in range(per_dev):
                kk = (n * both + h) * per_dev + k
                for j in range(CHUNK):
                    block = turn[h, pl.ds(j * per_dev + k, c_count, stride=mine), :].astype(jnp.bfloat16)
                    rhs_one[pl.ds(pl.multiple_of(kk * c_count, c_count), c_count), j * vir : (j + 1) * vir] = block
                    rhs_two[j * c_count : (j + 1) * c_count, pl.ds(pl.multiple_of(kk * vir, vir), vir)] = block


def cycle_step(w_all, x_all, rhs_one, rhs_two, exch, cyc, part_ref, col):
    cols, i_count, a_count, _ = x_all.shape
    cores = part_ref.shape[1]
    vir = part_ref.shape[4]
    c_count = vir // cols
    x_rows = i_count * a_count
    for o in range(cols):
        exch[o * x_rows : (o + 1) * x_rows, :] = lax.dot_general(
            x_all[o].reshape(x_rows, x_all.shape[3]), rhs_two[...], (((1,), (1,)), ((), ())),
            preferred_element_type=jnp.float32,
        )
    w_full = w_all[...].reshape(cols * x_rows, w_all.shape[3])
    own_lane = lax.broadcasted_iota(jnp.int32, (cols * x_rows, vir), 1) // c_count == col
    prod = jnp.dot(w_full, rhs_one[...], preferred_element_type=jnp.float32)
    gap = a_count + 8
    for j in range(CHUNK):
        tile = exch[:, (j // cols) * vir : (j // cols + 1) * vir]
        shift = lax.rem(col + cols - j % cols, cols) * c_count
        tile = pltpu.roll(tile, shift, 1)
        full = prod[:, j * vir : (j + 1) * vir] + jnp.where(own_lane, tile, 0.0)
        for i in range(cols * i_count):
            cyc[j, i * gap : i * gap + a_count, :] = full[i * a_count : (i + 1) * a_count]
    for a in range(a_count):
        for j in range(CHUNK):
            at = slice(j * i_count, (j + 1) * i_count)
            for o in range(cols):
                part_ref[o // cores, o % cores, a, at, :] = (
                    part_ref[o // cores, o % cores, a, at, :]
                    + cyc[j, pl.ds(o * i_count * gap + a, i_count, stride=gap), :]
                )


def fused_kernel(
    live_ref, occ_ref, vir_ref, row_ref, a_hbm, v_hbm, w_hbm, x_hbm, out_ref,
    vs, ab, a_own, w_own, w_split, w_mid, w_all, x_all, rhs_one, rhs_two, turn, part, cyc, exch, got_core, got_x, send_x, total,
    loc, loc_v, ss_up, ss_down, ss_row, rs_amp, ss_xg, rs_xg, ss_wg, rs_wg, ss_xc, rs_xc, ss_wc, rs_wc,
    ss_core, rs_core, ss_far, rs_far,
):
    f32, bf16 = jnp.float32, jnp.bfloat16
    depth, width = vs.shape
    zs, ys = lax.axis_size("grp"), lax.axis_size("row")
    cols = lax.axis_size("col")
    groups = zs * ys
    z, y, col = lax.axis_index("grp"), lax.axis_index("row"), lax.axis_index("col")
    grp = z * ys + y
    core, far = col % 2, col // 2
    vir = row_ref.shape[1]
    occ = occ_ref.shape[0]
    c_count = depth // vir
    a_count = width // vir
    chunks, all_rows = ab.shape[0], ab.shape[1]
    mine = all_rows // groups
    per_dev = mine // CHUNK
    i_count = occ // cols
    quarter = all_rows // cols
    edge = depth // live_ref.shape[0]

    def here(d_z=None, d_y=None, d_col=None):
        return (z if d_z is None else d_z, y if d_y is None else d_y, col if d_col is None else d_col)

    sibling = here(d_col=col + 1 - 2 * core)
    across = here(d_col=lax.rem(col + 2, cols))
    row_peer = here(d_y=1 - y)

    load_a = pltpu.make_async_copy(a_hbm, a_own, loc.at[0])
    load_a.start()
    load_w = pltpu.make_async_copy(w_hbm, w_own, loc.at[1])
    load_w.start()
    x_lanes = per_dev * vir
    own_x = pltpu.make_async_copy(
        x_hbm.at[:, pl.ds(pl.multiple_of(grp * a_count, a_count), a_count), :],
        x_all.at[col, :, :, pl.ds(pl.multiple_of(grp * x_lanes, x_lanes), x_lanes)],
        loc.at[2],
    )
    own_x.start()
    v_parts = loc_v.shape[0]
    v_rows = depth // v_parts

    def load_v(n):
        at = pl.ds(pl.multiple_of(n * v_rows, v_rows), v_rows)
        return pltpu.make_async_copy(v_hbm.at[at, :], vs.at[at, :], loc_v.at[n])

    for n in range(v_parts):
        load_v(n).start()

    barrier = pltpu.get_barrier_semaphore()

    def group_peer(d):
        other = lax.rem(grp + d, groups)
        return other, here(d_z=other // ys, d_y=other % ys)

    def col_peer(d):
        other = lax.rem(col + d, cols)
        return other, here(d_col=other)

    for d in range(1, groups):
        pl.semaphore_signal(barrier, inc=1, device_id=group_peer(d)[1], device_id_type=MESH)
    for d in range(1, cols):
        pl.semaphore_signal(barrier, inc=1, device_id=col_peer(d)[1], device_id_type=MESH)

    pl.semaphore_wait(barrier, groups - 1 + cols - 1)

    def send_xg(d):
        other, device = group_peer(d)
        return pltpu.make_async_remote_copy(
            src_ref=x_hbm.at[:, pl.ds(pl.multiple_of(other * a_count, a_count), a_count), :],
            dst_ref=x_all.at[col, :, :, pl.ds(pl.multiple_of(grp * x_lanes, x_lanes), x_lanes)],
            send_sem=ss_xg.at[d - 1],
            recv_sem=rs_xg.at[d - 1],
            device_id=device,
            device_id_type=MESH,
        )

    def send_wg(d):
        other, device = group_peer(d)
        return pltpu.make_async_remote_copy(
            src_ref=w_split.at[:, :, pl.ds(pl.multiple_of(other * a_count, a_count), a_count), :],
            dst_ref=w_mid.at[:, :, :, pl.ds(pl.multiple_of(grp * vir, vir), vir)],
            send_sem=ss_wg.at[d - 1],
            recv_sem=rs_wg.at[d - 1],
            device_id=device,
            device_id_type=MESH,
        )

    def amp(q, zz, yy, send, device):
        at = ab.at[q, pl.ds(pl.multiple_of((zz * ys + yy) * mine, mine), mine), :]
        return pltpu.make_async_remote_copy(
            src_ref=at,
            dst_ref=at,
            send_sem=send,
            recv_sem=rs_amp.at[q, zz * ys + yy],
            device_id=device,
            device_id_type=MESH,
        )

    def amp_up(q, zz):
        return amp(q, zz, y, ss_up.at[q, zz], here(d_z=lax.rem(z + 1, zs)))

    def amp_down(q, zz):
        return amp(q, zz, y, ss_down.at[q, zz], here(d_z=lax.rem(z + zs - 1, zs)))

    def amp_row(q, zz):
        return amp(q, zz, y, ss_row.at[q, zz], row_peer)

    def amp_wait(q, zz, yy):
        amp(q, zz, yy, ss_row.at[q, zz], row_peer).wait_recv()

    for d in range(1, groups):
        send_xg(d).start()

    def own_z(q):
        @pl.when(z < zs - 1)
        def _():
            amp_up(q, z).start()

        @pl.when(z > 0)
        def _():
            amp_down(q, z).start()

    load_w.wait()
    w_lanes = w_own.shape[2]
    come = lax.broadcasted_iota(jnp.int32, (w_lanes, w_lanes), 0)
    to = lax.broadcasted_iota(jnp.int32, (w_lanes, w_lanes), 1)
    t_owner, t_k, t_c = to // vir, (to % vir) // c_count, to % c_count
    pick = jnp.where(come == t_k * vir + t_owner * c_count + t_c, 1.0, 0.0).astype(bf16)

    @pl.loop(0, i_count // 2)
    def _(n):
        both = w_own[pl.ds(n * 2, 2)].reshape(2 * vir, w_lanes)
        moved = jnp.dot(both, pick, preferred_element_type=f32).astype(bf16)
        for q in range(cols):
            w_split[q, pl.ds(n * 2, 2)] = moved[:, q * vir : (q + 1) * vir].reshape(2, vir, vir)

    own_w = pltpu.make_async_copy(
        w_split.at[:, :, pl.ds(pl.multiple_of(grp * a_count, a_count), a_count), :],
        w_mid.at[:, :, :, pl.ds(pl.multiple_of(grp * vir, vir), vir)],
        loc.at[3],
    )
    own_w.start()

    load_a.wait()
    rows = a_own.shape[0]
    to = lax.broadcasted_iota(jnp.int32, (rows, rows), 0)
    come = lax.broadcasted_iota(jnp.int32, (rows, rows), 1)
    t_chunk, t_j, t_k = to // mine, (to % mine) // per_dev, to % per_dev
    pick = jnp.where(come == t_k * occ + t_chunk * CHUNK + t_j, 1.0, 0.0).astype(bf16)
    own_rows = pl.ds(pl.multiple_of(grp * mine, mine), mine)
    step = 512
    for n in range(depth // step):
        lanes = slice(n * step, (n + 1) * step)
        moved = jnp.dot(pick, a_own[:, lanes], preferred_element_type=f32).astype(bf16)
        for q in range(chunks):
            ab[q, own_rows, lanes] = moved[q * mine : (q + 1) * mine]

    early = 2

    @pl.loop(0, early)
    def _(q):
        own_z(q)

    @pl.loop(0, chunks)
    def _(q):
        amp_row(q, z).start()

    tiles = v_rows // edge

    @pl.loop(0, v_parts)
    def _(n):
        load_v(n).wait()

        @pl.loop(0, tiles)
        def _(m):
            k = n * tiles + m
            at = pl.ds(pl.multiple_of(k * edge, edge), edge)
            row = live_ref[pl.ds(k, 1), :].astype(f32)
            for b in range(width // edge):
                lanes = slice(b * edge, (b + 1) * edge)
                live = jnp.broadcast_to(row[:, b : b + 1], (edge, edge)).astype(bf16)
                vs[at, lanes] = vs[at, lanes] * live

    def forward(q, d):
        @pl.when(z - d >= 0)
        def _():
            amp_wait(q, z - d, y)

            @pl.when(z < zs - 1)
            def _():
                amp_up(q, z - d).start()

            amp_row(q, z - d).start()

        @pl.when(z + d < zs)
        def _():
            amp_wait(q, z + d, y)

            @pl.when(z > 0)
            def _():
                amp_down(q, z + d).start()

            amp_row(q, z + d).start()

    def wave(n):
        hops(n, range(zs - 1, 0, -1))

    def hops(n, which):
        for d in which:
            if isinstance(n, int):
                if 0 <= n - d < chunks:
                    forward(n - d, d)
            else:
                @pl.when(n - d < chunks)
                def _():
                    forward(n - d, d)

    def own(n):
        @pl.when(n < chunks)
        def _():
            own_z(n)

    ahead = zs

    wave(1)
    own(early)

    own_x.wait()
    for d in range(1, groups):
        send_xg(d).wait_recv()

    def send_xc(which, slot, device):
        return pltpu.make_async_remote_copy(
            src_ref=x_all.at[which],
            dst_ref=x_all.at[which],
            send_sem=ss_xc.at[slot],
            recv_sem=rs_xc.at[slot],
            device_id=device,
            device_id_type=MESH,
        )

    other_col = lax.rem(col + 2, cols)
    send_xc(col, 0, across).start()
    send_xc(col, 1, sibling).start()

    for d in range(1, groups):
        send_wg(d).start()
    wave(2)
    own(early + 1)

    own_w.wait()
    for d in range(1, groups):
        send_wg(d).wait_recv()

    def send_wc(d):
        other, device = col_peer(d)
        return pltpu.make_async_remote_copy(
            src_ref=w_mid.at[other],
            dst_ref=w_all.at[col],
            send_sem=ss_wc.at[d - 1],
            recv_sem=rs_wc.at[d - 1],
            device_id=device,
            device_id_type=MESH,
        )

    for d in range(1, cols):
        send_wc(d).start()
    w_all[col] = w_mid[col]

    for n in range(3, ahead):
        wave(n)
        own(early + n - 1)
    send_xc(other_col, 0, across).wait_recv()
    send_xc(other_col, 2, sibling).start()

    some = a_count // HALVES
    half = lambda h: pl.ds(h * some, some)
    send_core = lambda q, h: pltpu.make_async_remote_copy(
        src_ref=part.at[q % 2, :, 1 - core, half(h)],
        dst_ref=got_core.at[q, :, half(h)],
        send_sem=ss_core.at[q, h],
        recv_sem=rs_core.at[q, h],
        device_id=sibling,
        device_id_type=MESH,
    )
    send_far = lambda q, h: pltpu.make_async_remote_copy(
        src_ref=send_x.at[q % 2, half(h)],
        dst_ref=got_x.at[q, half(h)],
        send_sem=ss_far.at[q, h],
        recv_sem=rs_far.at[q, h],
        device_id=across,
        device_id_type=MESH,
    )

    def finish(q):
        slot = q % 2
        sub = lax.broadcasted_iota(jnp.int32, (i_count, vir), 0)
        occ_i = jnp.zeros((i_count, vir), f32)
        for i in range(i_count):
            occ_i = jnp.where(sub == i, occ_ref[col * i_count + i], occ_i)

        @pl.loop(0, HALVES)
        def _(h):
            send_far(q, h).wait_recv()
            for da in range(some):
                a = h * some + da
                base = vir_ref[grp * a_count + a] + row_ref[...] - occ_i
                for j in range(CHUNK):
                    at = slice(j * i_count, (j + 1) * i_count)
                    summed = part[slot, far, core, a, at, :] + got_core[q, far, a, at, :] + got_x[q, a, at, :]
                    to = pl.ds(pl.multiple_of((q * CHUNK + j) * i_count, i_count), i_count)
                    total[a, to, :] = summed / (base - occ_ref[q * CHUNK + j])

    @pl.loop(0, chunks)
    def _(q):
        slot = q % 2
        for zz in range(zs):
            amp_wait(q, zz, 1 - y)

        @pl.when(q >= 2)
        def _():
            for h in range(HALVES):
                send_core(q - 2, h).wait_send()

        hops(q + ahead, [zs - 1])
        ladder_step(ab.at[q], vs, part.at[slot], per_dev)
        hops(q + ahead, range(zs - 2, 0, -1))
        own(early + q + ahead - 1)
        turn_step(ab.at[q], turn, rhs_one, rhs_two, per_dev)

        @pl.when(q == 0)
        def _():
            send_xc(col, 1, sibling).wait_recv()
            send_xc(col, 2, sibling).wait_recv()
            for d in range(1, cols):
                send_wc(d).wait_recv()

        cycle_step(w_all, x_all, rhs_one, rhs_two, exch, cyc, part.at[slot], col)
        for h in range(HALVES):
            send_core(q, h).start()

        @pl.when(q >= 1)
        def _():
            finish(q - 1)

        @pl.loop(0, HALVES)
        def _(h):
            send_core(q, h).wait_recv()

            @pl.when(q >= 2)
            def _():
                send_far(q - 2, h).wait_send()

            at = half(h)
            send_x[slot, at] = part[slot, 1 - far, core, at] + got_core[q, 1 - far, at]
            send_far(q, h).start()

    finish(chunks - 1)

    for a in range(a_count):
        for i in range(i_count):
            block = total[a, pl.ds(i, occ, stride=i_count), :]
            out_ref[i * occ : (i + 1) * occ, a * vir : (a + 1) * vir] = block.astype(bf16)

    for d in range(1, groups):
        send_xg(d).wait_send()
        send_wg(d).wait_send()
    for d in range(1, cols):
        send_wc(d).wait_send()
    for slot in range(3):
        send_xc(col, slot, sibling).wait_send()

    @pl.loop(0, chunks)
    def _(q):
        for zz in range(zs):
            amp_row(q, zz).wait_send()

            @pl.when(jnp.logical_and(z < zs - 1, zz <= z))
            def _():
                amp_up(q, zz).wait_send()

            @pl.when(jnp.logical_and(z > 0, zz >= z))
            def _():
                amp_down(q, zz).wait_send()

    for q in range(chunks - 2, chunks):
        for h in range(HALVES):
            send_core(q, h).wait_send()
            send_far(q, h).wait_send()


def fused(amplitudes, ladder_ints, tile_live, cycle_direct, cycle_exchange, eps_occ, eps_vir):
    zs, ys, cols = lax.axis_size("grp"), lax.axis_size("row"), lax.axis_size("col")
    groups = zs * ys
    occ, vir = eps_occ.shape[0], eps_vir.shape[0]
    per_dev, i_count = occ // groups, occ // cols
    a_count, c_count = vir // groups, vir // cols
    depth, width = ladder_ints.shape
    chunks = occ // CHUNK
    mine = per_dev * CHUNK
    all_rows = groups * mine
    quarter = all_rows // cols
    f32, bf16 = jnp.float32, jnp.bfloat16
    dma = pltpu.SemaphoreType.DMA
    any_spec = pl.BlockSpec(memory_space=pl.ANY)
    smem = pl.BlockSpec(memory_space=pltpu.SMEM)
    vmem = pl.BlockSpec(memory_space=pltpu.VMEM)
    v_parts = 8
    return pl.pallas_call(
        fused_kernel,
        out_shape=jax.ShapeDtypeStruct((i_count * occ, width), bf16),
        in_specs=[vmem, smem, smem, vmem, any_spec, any_spec, any_spec, any_spec],
        out_specs=vmem,
        scratch_shapes=[
            pltpu.VMEM((depth, width), bf16),
            pltpu.VMEM((chunks, all_rows, depth), bf16),
            pltpu.VMEM((per_dev * occ, depth), bf16),
            pltpu.VMEM((i_count, vir, per_dev * vir), bf16),
            pltpu.VMEM((cols, i_count, vir, vir), bf16),
            pltpu.VMEM((cols, i_count, a_count, groups * vir), bf16),
            pltpu.VMEM((cols, i_count, a_count, groups * vir), bf16),
            pltpu.VMEM((cols, i_count, a_count, occ * vir), bf16),
            pltpu.VMEM((occ * c_count, CHUNK * vir), bf16),
            pltpu.VMEM((CHUNK * c_count, occ * vir), bf16),
            pltpu.VMEM((2, mine * c_count, vir), f32),
            pltpu.VMEM((2, cols // 2, 2, a_count, quarter, vir), f32),
            pltpu.VMEM((CHUNK, occ * (a_count + 8), vir), f32),
            pltpu.VMEM((occ * a_count, CHUNK * c_count), f32),
            pltpu.VMEM((chunks, cols // 2, a_count, quarter, vir), f32),
            pltpu.VMEM((chunks, a_count, quarter, vir), f32),
            pltpu.VMEM((2, a_count, quarter, vir), f32),
            pltpu.VMEM((a_count, i_count * occ, vir), f32),
            dma((4,)),
            dma((v_parts,)),
            dma((chunks, zs)),
            dma((chunks, zs)),
            dma((chunks, zs)),
            dma((chunks, groups)),
            dma((groups - 1,)),
            dma((groups - 1,)),
            dma((groups - 1,)),
            dma((groups - 1,)),
            dma((3,)),
            dma((3,)),
            dma((cols - 1,)),
            dma((cols - 1,)),
            dma((chunks, HALVES)),
            dma((chunks, HALVES)),
            dma((chunks, HALVES)),
            dma((chunks, HALVES)),
        ],
        compiler_params=pltpu.CompilerParams(collective_id=0, has_side_effects=True, vmem_limit_bytes=LIMIT),
    )(
        tile_live,
        eps_occ,
        eps_vir,
        eps_vir.reshape(1, vir),
        amplitudes,
        ladder_ints,
        cycle_direct.reshape(i_count, vir, per_dev * vir),
        cycle_exchange.reshape(i_count, vir, per_dev * vir),
    )


def cycle_kernel(t_ref, w_ref, x_ref, o_ref):
    occ, step, part, vir = t_ref.shape
    col = lax.axis_index("col")
    rows = w_ref.shape[0]
    u_one = jnp.concatenate(
        [t_ref[:, j].reshape(occ * part, vir) for j in range(step)], axis=1
    )
    direct = jnp.dot(w_ref[...], u_one, preferred_element_type=jnp.float32)
    u_two = jnp.concatenate(
        [t_ref[k].reshape(step * part, vir) for k in range(occ)], axis=1
    )
    exchange = lax.dot_general(
        x_ref[...], u_two, (((1,), (1,)), ((), ())), preferred_element_type=jnp.float32
    )
    own = lax.broadcasted_iota(jnp.int32, (rows, vir), 1) // part == col
    for j in range(step):
        piece = exchange[:, j * part : (j + 1) * part]
        piece = jnp.concatenate([piece] * (vir // part), axis=1)
        o_ref[j] = direct[:, j * vir : (j + 1) * vir] + jnp.where(own, piece, 0.0)


def cycle_sum(four, w, x):
    occ, _, part, vir = four.shape
    rows = w.shape[0]
    step = 8
    return pl.pallas_call(
        cycle_kernel,
        grid=(occ // step,),
        out_shape=jax.ShapeDtypeStruct((occ, rows, vir), jnp.float32),
        in_specs=[
            pl.BlockSpec((occ, step, part, vir), lambda n: (0, n, 0, 0)),
            pl.BlockSpec(w.shape, lambda n: (0, 0)),
            pl.BlockSpec(x.shape, lambda n: (0, 0)),
        ],
        out_specs=pl.BlockSpec((step, rows, vir), lambda n: (n, 0, 0)),
        compiler_params=pltpu.CompilerParams(vmem_limit_bytes=LIMIT),
    )(four, w, x)


def ladder_kernel(live_ref, a_ref, v_ref, o_ref, held):
    edge = v_ref.shape[0] // live_ref.shape[0]
    across = v_ref.shape[1] // edge
    n = pl.program_id(0)

    @pl.when(pl.program_id(1) == 0)
    def _():
        @pl.loop(0, live_ref.shape[0])
        def _(k):
            at = pl.ds(pl.multiple_of(k * edge, edge), edge)
            for b in range(across):
                lanes = slice(b * edge, (b + 1) * edge)
                live = live_ref[k, n * across + b].astype(jnp.float32)
                held[at, lanes] = (v_ref[at, lanes].astype(jnp.float32) * live).astype(jnp.bfloat16)

    o_ref[...] = jnp.dot(a_ref[...], held[...], preferred_element_type=jnp.float32)


def ladder_sum(amps, ints, live):
    rows, depth = amps.shape
    width = ints.shape[1]
    tall = 256
    wide = min(512, width)
    return pl.pallas_call(
        ladder_kernel,
        grid=(width // wide, rows // tall),
        out_shape=jax.ShapeDtypeStruct((rows, width), jnp.float32),
        in_specs=[
            pl.BlockSpec(memory_space=pltpu.SMEM),
            pl.BlockSpec((tall, depth), lambda n, m: (m, 0)),
            pl.BlockSpec((depth, wide), lambda n, m: (0, n)),
        ],
        out_specs=pl.BlockSpec((tall, wide), lambda n, m: (m, n)),
        scratch_shapes=[pltpu.VMEM((depth, wide), jnp.bfloat16)],
        compiler_params=pltpu.CompilerParams(vmem_limit_bytes=LIMIT),
    )(live, amps, ints)


def body(amplitudes, ladder_ints, tile_live, cycle_direct, cycle_exchange, eps_occ, eps_vir):
    groups = lax.axis_size(("grp", "row"))
    columns = lax.axis_size("col")
    col = lax.axis_index("col")
    grp = lax.axis_index(("grp", "row"))
    occ = eps_occ.shape[0]
    vir = eps_vir.shape[0]
    per_dev = occ // groups
    i_count = occ // columns
    a_count = vir // groups
    c_count = vir // columns
    f32 = jnp.float32

    x = cycle_exchange.reshape(i_count, groups, a_count, per_dev * vir)
    x = lax.all_to_all(x, ("grp", "row"), split_axis=1, concat_axis=3, tiled=True)
    x = lax.all_gather(x.reshape(i_count * a_count, occ * vir), "col", axis=0, tiled=True)

    w = cycle_direct.reshape(i_count, groups, a_count, per_dev, columns, c_count)
    w = w.transpose(1, 4, 0, 2, 3, 5).reshape(groups * columns, i_count * a_count, per_dev * c_count)
    w = lax.all_to_all(w, ("grp", "row", "col"), split_axis=0, concat_axis=0, tiled=True)
    w = w.reshape(groups, columns * i_count * a_count, per_dev * c_count)
    w = w.transpose(1, 0, 2).reshape(occ * a_count, occ * c_count)

    amps = lax.all_gather(amplitudes, ("grp", "row"), axis=0, tiled=True)
    ladder = ladder_sum(amps, ladder_ints, tile_live)
    amps, ladder = lax.optimization_barrier((amps, ladder))
    cycle = cycle_sum(amps.reshape(occ, occ, c_count, vir), w, x)
    cycle = cycle.reshape(occ, occ, a_count, vir).transpose(1, 0, 2, 3).reshape(occ * occ, a_count * vir)
    total = lax.psum_scatter(ladder + cycle, "col", scatter_dimension=0, tiled=True)

    occ_local = lax.dynamic_slice_in_dim(eps_occ, col * i_count, i_count)
    vir_local = lax.dynamic_slice_in_dim(eps_vir, grp * a_count, a_count)
    denom = (
        vir_local[None, None, :, None]
        + eps_vir[None, None, None, :]
        - occ_local[:, None, None, None]
        - eps_occ[None, :, None, None]
    ).reshape(i_count * occ, a_count * vir)
    return (total / denom).astype(jnp.bfloat16)


def solution(mesh):
    placed = (
        P(("grp", "row"), "col"),
        P("col", ("grp", "row")),
        P("col", ("grp", "row")),
        P("col", ("grp", "row")),
        P("col", ("grp", "row")),
        P(),
        P(),
    )
    fits = mesh.shape["row"] == 2 and mesh.shape["col"] == 4
    return jax.shard_map(
        fused if fits else body, mesh=mesh, in_specs=placed, out_specs=P("col", ("grp", "row")), check_vma=False
    )
```

```python
import functools

import jax
import jax.numpy as jnp
from jax import lax
from jax.experimental import pallas as pl
from jax.experimental.pallas import tpu as pltpu
from jax.sharding import PartitionSpec as P

LIMIT = 56 * 1024 * 1024
MESH = pl.DeviceIdType.MESH
HALVES = 2
CHUNK = 4


def ladder_step(a_ref, v_ref, part_ref, per_dev):
    cols, cores, _, quarter, vir = part_ref.shape
    mine = per_dev * CHUNK
    i_count = quarter // CHUNK

    prod = jnp.dot(a_ref[...], v_ref[...], preferred_element_type=jnp.float32)
    for o in range(cols * cores):
        for b in range(v_ref.shape[1] // vir):
            for h in range(i_count // per_dev):
                for j in range(CHUNK):
                    come = o * quarter + h * mine + j * per_dev
                    to = j * i_count + h * per_dev
                    part_ref[o // cores, o % cores, b, to : to + per_dev, :] = prod[
                        come : come + per_dev, b * vir : (b + 1) * vir
                    ]


def turn_step(a_ref, turn, rhs_one, rhs_two, per_dev):
    vir = turn.shape[2]
    mine = per_dev * CHUNK
    c_count = a_ref.shape[1] // vir
    both = turn.shape[0]

    @pl.loop(0, a_ref.shape[0] // mine // both)
    def _(n):
        for h in range(both):
            at = pl.ds(pl.multiple_of((n * both + h) * mine, mine), mine)
            for c in range(c_count):
                block = a_ref[at, c * vir : (c + 1) * vir].astype(jnp.float32)
                for r in range(0, mine, 8):
                    turn[h, c * mine + r : c * mine + r + 8, :] = block[r : r + 8]
            for k in range(per_dev):
                kk = (n * both + h) * per_dev + k
                for j in range(CHUNK):
                    block = turn[h, pl.ds(j * per_dev + k, c_count, stride=mine), :].astype(jnp.bfloat16)
                    rhs_one[pl.ds(pl.multiple_of(kk * c_count, c_count), c_count), j * vir : (j + 1) * vir] = block
                    rhs_two[j * c_count : (j + 1) * c_count, pl.ds(pl.multiple_of(kk * vir, vir), vir)] = block


def cycle_step(w_all, x_all, rhs_one, rhs_two, exch, cyc, part_ref, col):
    cols, i_count, a_count, _ = x_all.shape
    cores = part_ref.shape[1]
    vir = part_ref.shape[4]
    c_count = vir // cols
    x_rows = i_count * a_count
    for o in range(cols):
        exch[o * x_rows : (o + 1) * x_rows, :] = lax.dot_general(
            x_all[o].reshape(x_rows, x_all.shape[3]), rhs_two[...], (((1,), (1,)), ((), ())),
            preferred_element_type=jnp.float32,
        )
    w_full = w_all[...].reshape(cols * x_rows, w_all.shape[3])
    own_lane = lax.broadcasted_iota(jnp.int32, (cols * x_rows, vir), 1) // c_count == col
    prod = jnp.dot(w_full, rhs_one[...], preferred_element_type=jnp.float32)
    gap = a_count + 8
    for j in range(CHUNK):
        tile = exch[:, (j // cols) * vir : (j // cols + 1) * vir]
        shift = lax.rem(col + cols - j % cols, cols) * c_count
        tile = pltpu.roll(tile, shift, 1)
        full = prod[:, j * vir : (j + 1) * vir] + jnp.where(own_lane, tile, 0.0)
        for i in range(cols * i_count):
            cyc[j, i * gap : i * gap + a_count, :] = full[i * a_count : (i + 1) * a_count]
    for a in range(a_count):
        for j in range(CHUNK):
            at = slice(j * i_count, (j + 1) * i_count)
            for o in range(cols):
                part_ref[o // cores, o % cores, a, at, :] = (
                    part_ref[o // cores, o % cores, a, at, :]
                    + cyc[j, pl.ds(o * i_count * gap + a, i_count, stride=gap), :]
                )


def fused_kernel(
    live_ref, occ_ref, vir_ref, row_ref, a_hbm, v_hbm, w_hbm, x_hbm, out_ref,
    vs, ab, a_own, w_own, w_split, w_mid, w_all, x_all, rhs_one, rhs_two, turn, part, cyc, exch, got_core, got_x, send_x, total,
    loc, loc_v, ss_up, ss_down, ss_row, rs_amp, ss_xg, rs_xg, ss_wg, rs_wg, ss_xc, rs_xc, ss_wc, rs_wc,
    ss_core, rs_core, ss_far, rs_far,
):
    f32, bf16 = jnp.float32, jnp.bfloat16
    depth, width = vs.shape
    zs, ys = lax.axis_size("grp"), lax.axis_size("row")
    cols = lax.axis_size("col")
    groups = zs * ys
    z, y, col = lax.axis_index("grp"), lax.axis_index("row"), lax.axis_index("col")
    grp = z * ys + y
    core, far = col % 2, col // 2
    vir = row_ref.shape[1]
    occ = occ_ref.shape[0]
    c_count = depth // vir
    a_count = width // vir
    chunks, all_rows = ab.shape[0], ab.shape[1]
    mine = all_rows // groups
    per_dev = mine // CHUNK
    i_count = occ // cols
    quarter = all_rows // cols
    edge = depth // live_ref.shape[0]

    def here(d_z=None, d_y=None, d_col=None):
        return (z if d_z is None else d_z, y if d_y is None else d_y, col if d_col is None else d_col)

    sibling = here(d_col=col + 1 - 2 * core)
    across = here(d_col=lax.rem(col + 2, cols))
    row_peer = here(d_y=1 - y)

    load_a = pltpu.make_async_copy(a_hbm, a_own, loc.at[0])
    load_a.start()
    load_w = pltpu.make_async_copy(w_hbm, w_own, loc.at[1])
    load_w.start()
    x_lanes = per_dev * vir
    own_x = pltpu.make_async_copy(
        x_hbm.at[:, pl.ds(pl.multiple_of(grp * a_count, a_count), a_count), :],
        x_all.at[col, :, :, pl.ds(pl.multiple_of(grp * x_lanes, x_lanes), x_lanes)],
        loc.at[2],
    )
    own_x.start()
    v_parts = loc_v.shape[0]
    v_rows = depth // v_parts

    def load_v(n):
        at = pl.ds(pl.multiple_of(n * v_rows, v_rows), v_rows)
        return pltpu.make_async_copy(v_hbm.at[at, :], vs.at[at, :], loc_v.at[n])

    for n in range(v_parts):
        load_v(n).start()

    barrier = pltpu.get_barrier_semaphore()

    def group_peer(d):
        other = lax.rem(grp + d, groups)
        return other, here(d_z=other // ys, d_y=other % ys)

    def col_peer(d):
        other = lax.rem(col + d, cols)
        return other, here(d_col=other)

    for d in range(1, groups):
        pl.semaphore_signal(barrier, inc=1, device_id=group_peer(d)[1], device_id_type=MESH)
    for d in range(1, cols):
        pl.semaphore_signal(barrier, inc=1, device_id=col_peer(d)[1], device_id_type=MESH)

    pl.semaphore_wait(barrier, groups - 1 + cols - 1)

    def send_xg(d):
        other, device = group_peer(d)
        return pltpu.make_async_remote_copy(
            src_ref=x_hbm.at[:, pl.ds(pl.multiple_of(other * a_count, a_count), a_count), :],
            dst_ref=x_all.at[col, :, :, pl.ds(pl.multiple_of(grp * x_lanes, x_lanes), x_lanes)],
            send_sem=ss_xg.at[d - 1],
            recv_sem=rs_xg.at[d - 1],
            device_id=device,
            device_id_type=MESH,
        )

    def send_wg(d):
        other, device = group_peer(d)
        return pltpu.make_async_remote_copy(
            src_ref=w_split.at[:, :, pl.ds(pl.multiple_of(other * a_count, a_count), a_count), :],
            dst_ref=w_mid.at[:, :, :, pl.ds(pl.multiple_of(grp * vir, vir), vir)],
            send_sem=ss_wg.at[d - 1],
            recv_sem=rs_wg.at[d - 1],
            device_id=device,
            device_id_type=MESH,
        )

    def amp(q, zz, yy, send, device):
        at = ab.at[q, pl.ds(pl.multiple_of((zz * ys + yy) * mine, mine), mine), :]
        return pltpu.make_async_remote_copy(
            src_ref=at,
            dst_ref=at,
            send_sem=send,
            recv_sem=rs_amp.at[q, zz * ys + yy],
            device_id=device,
            device_id_type=MESH,
        )

    def amp_up(q, zz):
        return amp(q, zz, y, ss_up.at[q, zz], here(d_z=lax.rem(z + 1, zs)))

    def amp_down(q, zz):
        return amp(q, zz, y, ss_down.at[q, zz], here(d_z=lax.rem(z + zs - 1, zs)))

    def amp_row(q, zz):
        return amp(q, zz, y, ss_row.at[q, zz], row_peer)

    def amp_wait(q, zz, yy):
        amp(q, zz, yy, ss_row.at[q, zz], row_peer).wait_recv()

    for d in range(1, groups):
        send_xg(d).start()

    def own_z(q):
        @pl.when(z < zs - 1)
        def _():
            amp_up(q, z).start()

        @pl.when(z > 0)
        def _():
            amp_down(q, z).start()

    load_w.wait()
    w_lanes = w_own.shape[2]
    come = lax.broadcasted_iota(jnp.int32, (w_lanes, w_lanes), 0)
    to = lax.broadcasted_iota(jnp.int32, (w_lanes, w_lanes), 1)
    t_owner, t_k, t_c = to // vir, (to % vir) // c_count, to % c_count
    pick = jnp.where(come == t_k * vir + t_owner * c_count + t_c, 1.0, 0.0).astype(bf16)

    @pl.loop(0, i_count // 2)
    def _(n):
        both = w_own[pl.ds(n * 2, 2)].reshape(2 * vir, w_lanes)
        moved = jnp.dot(both, pick, preferred_element_type=f32).astype(bf16)
        for q in range(cols):
            w_split[q, pl.ds(n * 2, 2)] = moved[:, q * vir : (q + 1) * vir].reshape(2, vir, vir)

    own_w = pltpu.make_async_copy(
        w_split.at[:, :, pl.ds(pl.multiple_of(grp * a_count, a_count), a_count), :],
        w_mid.at[:, :, :, pl.ds(pl.multiple_of(grp * vir, vir), vir)],
        loc.at[3],
    )
    own_w.start()

    load_a.wait()
    rows = a_own.shape[0]
    to = lax.broadcasted_iota(jnp.int32, (rows, rows), 0)
    come = lax.broadcasted_iota(jnp.int32, (rows, rows), 1)
    t_chunk, t_j, t_k = to // mine, (to % mine) // per_dev, to % per_dev
    pick = jnp.where(come == t_k * occ + t_chunk * CHUNK + t_j, 1.0, 0.0).astype(bf16)
    own_rows = pl.ds(pl.multiple_of(grp * mine, mine), mine)
    step = 512
    for n in range(depth // step):
        lanes = slice(n * step, (n + 1) * step)
        moved = jnp.dot(pick, a_own[:, lanes], preferred_element_type=f32).astype(bf16)
        for q in range(chunks):
            ab[q, own_rows, lanes] = moved[q * mine : (q + 1) * mine]

    early = 2

    @pl.loop(0, early)
    def _(q):
        own_z(q)

    @pl.loop(0, chunks)
    def _(q):
        amp_row(q, z).start()

    tiles = v_rows // edge

    @pl.loop(0, v_parts)
    def _(n):
        load_v(n).wait()

        @pl.loop(0, tiles)
        def _(m):
            k = n * tiles + m
            at = pl.ds(pl.multiple_of(k * edge, edge), edge)
            row = live_ref[pl.ds(k, 1), :].astype(f32)
            for b in range(width // edge):
                lanes = slice(b * edge, (b + 1) * edge)
                live = jnp.broadcast_to(row[:, b : b + 1], (edge, edge)).astype(bf16)
                vs[at, lanes] = vs[at, lanes] * live

    def forward(q, d):
        @pl.when(z - d >= 0)
        def _():
            amp_wait(q, z - d, y)

            @pl.when(z < zs - 1)
            def _():
                amp_up(q, z - d).start()

            amp_row(q, z - d).start()

        @pl.when(z + d < zs)
        def _():
            amp_wait(q, z + d, y)

            @pl.when(z > 0)
            def _():
                amp_down(q, z + d).start()

            amp_row(q, z + d).start()

    def wave(n):
        hops(n, range(zs - 1, 0, -1))

    def hops(n, which):
        for d in which:
            if isinstance(n, int):
                if 0 <= n - d < chunks:
                    forward(n - d, d)
            else:
                @pl.when(n - d < chunks)
                def _():
                    forward(n - d, d)

    def own(n):
        @pl.when(n < chunks)
        def _():
            own_z(n)

    ahead = zs

    wave(1)
    own(early)

    own_x.wait()
    for d in range(1, groups):
        send_xg(d).wait_recv()

    def send_xc(which, slot, device):
        return pltpu.make_async_remote_copy(
            src_ref=x_all.at[which],
            dst_ref=x_all.at[which],
            send_sem=ss_xc.at[slot],
            recv_sem=rs_xc.at[slot],
            device_id=device,
            device_id_type=MESH,
        )

    other_col = lax.rem(col + 2, cols)
    send_xc(col, 0, across).start()
    send_xc(col, 1, sibling).start()

    for d in range(1, groups):
        send_wg(d).start()
    wave(2)
    own(early + 1)

    own_w.wait()
    for d in range(1, groups):
        send_wg(d).wait_recv()

    def send_wc(d):
        other, device = col_peer(d)
        return pltpu.make_async_remote_copy(
            src_ref=w_mid.at[other],
            dst_ref=w_all.at[col],
            send_sem=ss_wc.at[d - 1],
            recv_sem=rs_wc.at[d - 1],
            device_id=device,
            device_id_type=MESH,
        )

    for d in range(1, cols):
        send_wc(d).start()
    w_all[col] = w_mid[col]

    for n in range(3, ahead):
        wave(n)
        own(early + n - 1)
    send_xc(other_col, 0, across).wait_recv()
    send_xc(other_col, 2, sibling).start()

    some = a_count // HALVES
    half = lambda h: pl.ds(h * some, some)
    send_core = lambda q, h: pltpu.make_async_remote_copy(
        src_ref=part.at[q % 2, :, 1 - core, half(h)],
        dst_ref=got_core.at[q, :, half(h)],
        send_sem=ss_core.at[q, h],
        recv_sem=rs_core.at[q, h],
        device_id=sibling,
        device_id_type=MESH,
    )
    send_far = lambda q, h: pltpu.make_async_remote_copy(
        src_ref=send_x.at[q % 2, half(h)],
        dst_ref=got_x.at[q, half(h)],
        send_sem=ss_far.at[q, h],
        recv_sem=rs_far.at[q, h],
        device_id=across,
        device_id_type=MESH,
    )

    def finish(q):
        slot = q % 2
        sub = lax.broadcasted_iota(jnp.int32, (i_count, vir), 0)
        occ_i = jnp.zeros((i_count, vir), f32)
        for i in range(i_count):
            occ_i = jnp.where(sub == i, occ_ref[col * i_count + i], occ_i)

        @pl.loop(0, HALVES)
        def _(h):
            send_far(q, h).wait_recv()
            for da in range(some):
                a = h * some + da
                base = vir_ref[grp * a_count + a] + row_ref[...] - occ_i
                for j in range(CHUNK):
                    at = slice(j * i_count, (j + 1) * i_count)
                    summed = part[slot, far, core, a, at, :] + got_core[q, far, a, at, :] + got_x[q, a, at, :]
                    to = pl.ds(pl.multiple_of((q * CHUNK + j) * i_count, i_count), i_count)
                    total[a, to, :] = summed / (base - occ_ref[q * CHUNK + j])

    @pl.loop(0, chunks)
    def _(q):
        slot = q % 2
        for zz in range(zs):
            amp_wait(q, zz, 1 - y)

        @pl.when(q >= 2)
        def _():
            for h in range(HALVES):
                send_core(q - 2, h).wait_send()

        hops(q + ahead, [zs - 1])
        ladder_step(ab.at[q], vs, part.at[slot], per_dev)
        hops(q + ahead, range(zs - 2, 1, -1))
        turn_step(ab.at[q], turn, rhs_one, rhs_two, per_dev)

        hops(q + ahead, [1])
        own(early + q + ahead - 1)

        @pl.when(q == 0)
        def _():
            send_xc(col, 1, sibling).wait_recv()
            send_xc(col, 2, sibling).wait_recv()
            for d in range(1, cols):
                send_wc(d).wait_recv()

        cycle_step(w_all, x_all, rhs_one, rhs_two, exch, cyc, part.at[slot], col)
        for h in range(HALVES):
            send_core(q, h).start()

        @pl.when(q >= 1)
        def _():
            finish(q - 1)

        @pl.loop(0, HALVES)
        def _(h):
            send_core(q, h).wait_recv()

            @pl.when(q >= 2)
            def _():
                send_far(q - 2, h).wait_send()

            at = half(h)
            send_x[slot, at] = part[slot, 1 - far, core, at] + got_core[q, 1 - far, at]
            send_far(q, h).start()

    finish(chunks - 1)

    for a in range(a_count):
        for i in range(i_count):
            block = total[a, pl.ds(i, occ, stride=i_count), :]
            out_ref[i * occ : (i + 1) * occ, a * vir : (a + 1) * vir] = block.astype(bf16)

    for d in range(1, groups):
        send_xg(d).wait_send()
        send_wg(d).wait_send()
    for d in range(1, cols):
        send_wc(d).wait_send()
    for slot in range(3):
        send_xc(col, slot, sibling).wait_send()

    @pl.loop(0, chunks)
    def _(q):
        for zz in range(zs):
            amp_row(q, zz).wait_send()

            @pl.when(jnp.logical_and(z < zs - 1, zz <= z))
            def _():
                amp_up(q, zz).wait_send()

            @pl.when(jnp.logical_and(z > 0, zz >= z))
            def _():
                amp_down(q, zz).wait_send()

    for q in range(chunks - 2, chunks):
        for h in range(HALVES):
            send_core(q, h).wait_send()
            send_far(q, h).wait_send()


def fused(amplitudes, ladder_ints, tile_live, cycle_direct, cycle_exchange, eps_occ, eps_vir):
    zs, ys, cols = lax.axis_size("grp"), lax.axis_size("row"), lax.axis_size("col")
    groups = zs * ys
    occ, vir = eps_occ.shape[0], eps_vir.shape[0]
    per_dev, i_count = occ // groups, occ // cols
    a_count, c_count = vir // groups, vir // cols
    depth, width = ladder_ints.shape
    chunks = occ // CHUNK
    mine = per_dev * CHUNK
    all_rows = groups * mine
    quarter = all_rows // cols
    f32, bf16 = jnp.float32, jnp.bfloat16
    dma = pltpu.SemaphoreType.DMA
    any_spec = pl.BlockSpec(memory_space=pl.ANY)
    smem = pl.BlockSpec(memory_space=pltpu.SMEM)
    vmem = pl.BlockSpec(memory_space=pltpu.VMEM)
    v_parts = 8
    return pl.pallas_call(
        fused_kernel,
        out_shape=jax.ShapeDtypeStruct((i_count * occ, width), bf16),
        in_specs=[vmem, smem, smem, vmem, any_spec, any_spec, any_spec, any_spec],
        out_specs=vmem,
        scratch_shapes=[
            pltpu.VMEM((depth, width), bf16),
            pltpu.VMEM((chunks, all_rows, depth), bf16),
            pltpu.VMEM((per_dev * occ, depth), bf16),
            pltpu.VMEM((i_count, vir, per_dev * vir), bf16),
            pltpu.VMEM((cols, i_count, vir, vir), bf16),
            pltpu.VMEM((cols, i_count, a_count, groups * vir), bf16),
            pltpu.VMEM((cols, i_count, a_count, groups * vir), bf16),
            pltpu.VMEM((cols, i_count, a_count, occ * vir), bf16),
            pltpu.VMEM((occ * c_count, CHUNK * vir), bf16),
            pltpu.VMEM((CHUNK * c_count, occ * vir), bf16),
            pltpu.VMEM((2, mine * c_count, vir), f32),
            pltpu.VMEM((2, cols // 2, 2, a_count, quarter, vir), f32),
            pltpu.VMEM((CHUNK, occ * (a_count + 8), vir), f32),
            pltpu.VMEM((occ * a_count, CHUNK * c_count), f32),
            pltpu.VMEM((chunks, cols // 2, a_count, quarter, vir), f32),
            pltpu.VMEM((chunks, a_count, quarter, vir), f32),
            pltpu.VMEM((2, a_count, quarter, vir), f32),
            pltpu.VMEM((a_count, i_count * occ, vir), f32),
            dma((4,)),
            dma((v_parts,)),
            dma((chunks, zs)),
            dma((chunks, zs)),
            dma((chunks, zs)),
            dma((chunks, groups)),
            dma((groups - 1,)),
            dma((groups - 1,)),
            dma((groups - 1,)),
            dma((groups - 1,)),
            dma((3,)),
            dma((3,)),
            dma((cols - 1,)),
            dma((cols - 1,)),
            dma((chunks, HALVES)),
            dma((chunks, HALVES)),
            dma((chunks, HALVES)),
            dma((chunks, HALVES)),
        ],
        compiler_params=pltpu.CompilerParams(collective_id=0, has_side_effects=True, vmem_limit_bytes=LIMIT),
    )(
        tile_live,
        eps_occ,
        eps_vir,
        eps_vir.reshape(1, vir),
        amplitudes,
        ladder_ints,
        cycle_direct.reshape(i_count, vir, per_dev * vir),
        cycle_exchange.reshape(i_count, vir, per_dev * vir),
    )


def cycle_kernel(t_ref, w_ref, x_ref, o_ref):
    occ, step, part, vir = t_ref.shape
    col = lax.axis_index("col")
    rows = w_ref.shape[0]
    u_one = jnp.concatenate(
        [t_ref[:, j].reshape(occ * part, vir) for j in range(step)], axis=1
    )
    direct = jnp.dot(w_ref[...], u_one, preferred_element_type=jnp.float32)
    u_two = jnp.concatenate(
        [t_ref[k].reshape(step * part, vir) for k in range(occ)], axis=1
    )
    exchange = lax.dot_general(
        x_ref[...], u_two, (((1,), (1,)), ((), ())), preferred_element_type=jnp.float32
    )
    own = lax.broadcasted_iota(jnp.int32, (rows, vir), 1) // part == col
    for j in range(step):
        piece = exchange[:, j * part : (j + 1) * part]
        piece = jnp.concatenate([piece] * (vir // part), axis=1)
        o_ref[j] = direct[:, j * vir : (j + 1) * vir] + jnp.where(own, piece, 0.0)


def cycle_sum(four, w, x):
    occ, _, part, vir = four.shape
    rows = w.shape[0]
    step = 8
    return pl.pallas_call(
        cycle_kernel,
        grid=(occ // step,),
        out_shape=jax.ShapeDtypeStruct((occ, rows, vir), jnp.float32),
        in_specs=[
            pl.BlockSpec((occ, step, part, vir), lambda n: (0, n, 0, 0)),
            pl.BlockSpec(w.shape, lambda n: (0, 0)),
            pl.BlockSpec(x.shape, lambda n: (0, 0)),
        ],
        out_specs=pl.BlockSpec((step, rows, vir), lambda n: (n, 0, 0)),
        compiler_params=pltpu.CompilerParams(vmem_limit_bytes=LIMIT),
    )(four, w, x)


def ladder_kernel(live_ref, a_ref, v_ref, o_ref, held):
    edge = v_ref.shape[0] // live_ref.shape[0]
    across = v_ref.shape[1] // edge
    n = pl.program_id(0)

    @pl.when(pl.program_id(1) == 0)
    def _():
        @pl.loop(0, live_ref.shape[0])
        def _(k):
            at = pl.ds(pl.multiple_of(k * edge, edge), edge)
            for b in range(across):
                lanes = slice(b * edge, (b + 1) * edge)
                live = live_ref[k, n * across + b].astype(jnp.float32)
                held[at, lanes] = (v_ref[at, lanes].astype(jnp.float32) * live).astype(jnp.bfloat16)

    o_ref[...] = jnp.dot(a_ref[...], held[...], preferred_element_type=jnp.float32)


def ladder_sum(amps, ints, live):
    rows, depth = amps.shape
    width = ints.shape[1]
    tall = 256
    wide = min(512, width)
    return pl.pallas_call(
        ladder_kernel,
        grid=(width // wide, rows // tall),
        out_shape=jax.ShapeDtypeStruct((rows, width), jnp.float32),
        in_specs=[
            pl.BlockSpec(memory_space=pltpu.SMEM),
            pl.BlockSpec((tall, depth), lambda n, m: (m, 0)),
            pl.BlockSpec((depth, wide), lambda n, m: (0, n)),
        ],
        out_specs=pl.BlockSpec((tall, wide), lambda n, m: (m, n)),
        scratch_shapes=[pltpu.VMEM((depth, wide), jnp.bfloat16)],
        compiler_params=pltpu.CompilerParams(vmem_limit_bytes=LIMIT),
    )(live, amps, ints)


def body(amplitudes, ladder_ints, tile_live, cycle_direct, cycle_exchange, eps_occ, eps_vir):
    groups = lax.axis_size(("grp", "row"))
    columns = lax.axis_size("col")
    col = lax.axis_index("col")
    grp = lax.axis_index(("grp", "row"))
    occ = eps_occ.shape[0]
    vir = eps_vir.shape[0]
    per_dev = occ // groups
    i_count = occ // columns
    a_count = vir // groups
    c_count = vir // columns
    f32 = jnp.float32

    x = cycle_exchange.reshape(i_count, groups, a_count, per_dev * vir)
    x = lax.all_to_all(x, ("grp", "row"), split_axis=1, concat_axis=3, tiled=True)
    x = lax.all_gather(x.reshape(i_count * a_count, occ * vir), "col", axis=0, tiled=True)

    w = cycle_direct.reshape(i_count, groups, a_count, per_dev, columns, c_count)
    w = w.transpose(1, 4, 0, 2, 3, 5).reshape(groups * columns, i_count * a_count, per_dev * c_count)
    w = lax.all_to_all(w, ("grp", "row", "col"), split_axis=0, concat_axis=0, tiled=True)
    w = w.reshape(groups, columns * i_count * a_count, per_dev * c_count)
    w = w.transpose(1, 0, 2).reshape(occ * a_count, occ * c_count)

    amps = lax.all_gather(amplitudes, ("grp", "row"), axis=0, tiled=True)
    ladder = ladder_sum(amps, ladder_ints, tile_live)
    amps, ladder = lax.optimization_barrier((amps, ladder))
    cycle = cycle_sum(amps.reshape(occ, occ, c_count, vir), w, x)
    cycle = cycle.reshape(occ, occ, a_count, vir).transpose(1, 0, 2, 3).reshape(occ * occ, a_count * vir)
    total = lax.psum_scatter(ladder + cycle, "col", scatter_dimension=0, tiled=True)

    occ_local = lax.dynamic_slice_in_dim(eps_occ, col * i_count, i_count)
    vir_local = lax.dynamic_slice_in_dim(eps_vir, grp * a_count, a_count)
    denom = (
        vir_local[None, None, :, None]
        + eps_vir[None, None, None, :]
        - occ_local[:, None, None, None]
        - eps_occ[None, :, None, None]
    ).reshape(i_count * occ, a_count * vir)
    return (total / denom).astype(jnp.bfloat16)


def solution(mesh):
    placed = (
        P(("grp", "row"), "col"),
        P("col", ("grp", "row")),
        P("col", ("grp", "row")),
        P("col", ("grp", "row")),
        P("col", ("grp", "row")),
        P(),
        P(),
    )
    fits = mesh.shape["row"] == 2 and mesh.shape["col"] == 4
    return jax.shard_map(
        fused if fits else body, mesh=mesh, in_specs=placed, out_specs=P("col", ("grp", "row")), check_vma=False
    )
```
